512 devices in a mesh: gx: 32 (over x, y, core), gy: 16 (over z).
Axes of the slice: x: 4, y: 4, z: 16, core: 2. Of those that a mesh axis runs over, the one named last changes fastest.
Arguments:
- right_side: float32 [4096, 2048], P('gx', 'gy'), may hold values from -6 to 6
- shift: float32 [4096, 2048], P('gx', 'gy'), may hold values from 0.02 to 0.5
- face_x: float32 [4096, 2048], P('gx', 'gy'), may hold values from 0.3 to 5
- face_y: float32 [4096, 2048], P('gx', 'gy'), may hold values from 0.3 to 5
- ice_mask: int32 [4096, 2048], P('gx', 'gy'), may hold values 0 or 1
- deflation: float32 [32, 4096, 2048], P(None, 'gx', 'gy'), may hold values from -6 to 6
- coarse_matrix: float32 [16, 1024, 1024], P('gy', 'gx'), as said below
Outputs:
- solution_field: float32 [4096, 2048], P('gx', 'gy')
- residual: float32 [4096, 2048], P('gx', 'gy')
The draws below stay inside these ranges and needn't reach their ends.
Inputs may be any that keep to these rules, and one draw needn't show every extreme that they name: Each coarse_matrix[b] is symmetric positive definite.
All inputs are finite; a program needn't handle non-finite values. No bound on the sum of `ice_mask` on one device may be relied on, other than what follows from the above.
Results may differ from the reference program's by a relative error of at most 0.0023.
Values sent between devices are 32-bit elements; how exact they have to be, the bound alone decides.
A program may use at most 64 MiB of HBM per device.

```python
import math
import jax
import jax.numpy as jnp
from jax import lax

CX = 128
CY = 128
K = 32
ITERS = 3
NX = 4096
NY = 2048
COARSE = 1024
GROUPS = 16
N_GX = 32
N_GY = 16


def draw_coarse_matrix(key, part):
    scale = 12.0 * math.sqrt(K * CX * CY)
    inner_rank = max(COARSE // 4, 1)
    key_diag, key_raw = jax.random.split(key, 2)
    diag_vals = jnp.exp(jax.random.uniform(key_diag, (GROUPS, COARSE), jnp.float32, math.log(0.01), math.log(4.0)))
    raw = jax.random.normal(key_raw, (GROUPS, COARSE, inner_rank), jnp.float32)
    gram = jnp.einsum('gir,gjr->gij', raw, raw, precision=lax.Precision.HIGHEST) / inner_rank
    gram = 0.5 * (gram + jnp.swapaxes(gram, 1, 2))
    unit = jnp.eye(COARSE, dtype=jnp.float32)[None, :, :]
    return (gram + diag_vals[:, :, None] * unit) * scale


def with_ends(array, rng, least, high):
    place = [jax.random.randint(jax.random.fold_in(rng, axis), (), 0, length) for axis, length in enumerate(array.shape)]
    longest = array.shape.index(max(array.shape))
    beside = place[:longest] + [(place[longest] + 1) % array.shape[longest]] + place[longest + 1:]
    return array.at[tuple(place)].set(least).at[tuple(beside)].set(high)


def level_of(key, dims, cuts, smallest, top_value):
    gain = 1.0
    for axis_at, parts in cuts:
        steps = jax.random.uniform(jax.random.fold_in(jax.random.fold_in(key, 6), axis_at), (parts,), jnp.float32, smallest / len(cuts), top_value / len(cuts))
        gain = gain * jnp.repeat(jnp.exp(steps), dims[axis_at] // parts).reshape((-1,) + (1,) * (len(dims) - 1 - axis_at))
    return gain


def gaussian(key, shape, width, most, cuts=(), held_as=jnp.bfloat16):
    values = jax.random.normal(key, shape, jnp.float32) * width
    if len(cuts) > 0:
        values = level_of(key, shape, cuts, -0.22, 0.18) * values
    return jnp.clip(values, min=-most, max=most).astype(held_as)


def setup_inputs(seed: int = 0) -> dict:
    seeds = jax.random.split(jax.random.key(seed), 8)
    return {
        "right_side": gaussian(seeds[0], (NX, NY), 1.0, 6.0, ((0, 32), (1, 16)), jnp.float32),
        "shift": jnp.clip(jnp.exp(math.log(0.5) - 3.218876 * jax.random.uniform(seeds[1], (NX, NY), jnp.float32) ** level_of(seeds[1], (NX, NY), ((0, 32), (1, 16)), -0.2, 0.2)), 0.02, 0.5),
        "face_x": jnp.clip(jnp.exp(math.log(5.0) - 2.8134107 * jax.random.uniform(seeds[2], (NX, NY), jnp.float32) ** level_of(seeds[2], (NX, NY), ((0, 32), (1, 16)), -0.2, 0.2)), 0.3, 5.0),
        "face_y": jnp.clip(jnp.exp(math.log(5.0) - 2.8134107 * jax.random.uniform(seeds[3], (NX, NY), jnp.float32) ** level_of(seeds[3], (NX, NY), ((0, 32), (1, 16)), -0.2, 0.2)), 0.3, 5.0),
        "ice_mask": with_ends((jax.random.randint(seeds[4], (NX, NY), 0, 4) < 3).astype(jnp.int32), jax.random.fold_in(seeds[4], 1), 0, 1),
        "deflation": gaussian(seeds[5], (K, NX, NY), 1.0, 6.0, ((1, 32), (2, 16)), jnp.float32),
        "coarse_matrix": draw_coarse_matrix(jax.random.fold_in(seeds[7], 71), 0),
    }


def operate(field, self_term, coef_x, coef_up, coef_y, coef_left):
    padded = jnp.pad(field, 1)
    below = padded[2:, 1:-1]
    above = padded[:-2, 1:-1]
    right = padded[1:-1, 2:]
    leftv = padded[1:-1, :-2]
    return self_term * field + coef_x * (field - below) + coef_up * (field - above) + coef_y * (field - right) + coef_left * (field - leftv)

def reference(right_side, shift, face_x, face_y, ice_mask, deflation, coarse_matrix):
    high = lax.Precision.HIGHEST
    mask = ice_mask.astype(right_side.dtype)
    coef_x = face_x * mask
    coef_y = face_y * mask
    coef_up = jnp.concatenate([jnp.zeros_like(coef_x[:1]), coef_x[:-1]], axis=0)
    coef_left = jnp.concatenate([jnp.zeros_like(coef_y[:, :1]), coef_y[:, :-1]], axis=1)
    self_term = shift * mask + (1.0 - mask)
    diag_a = self_term + coef_x + coef_up + coef_y + coef_left
    blocks = deflation.reshape(K, N_GX, CX, N_GY, CY)
    factors = jnp.linalg.cholesky(coarse_matrix)

    def precondition(field):
        tiles = field.reshape(N_GX, CX, N_GY, CY)
        coeffs = jnp.einsum('kaxby,axby->bak', blocks, tiles, precision=high).reshape(N_GY, COARSE)
        solved = lax.map(lambda pair: jax.scipy.linalg.cho_solve((pair[0], True), pair[1]), (factors, coeffs))
        solved = solved.reshape(N_GY, N_GX, K)
        back = jnp.einsum('kaxby,bak->axby', blocks, solved, precision=high).reshape(NX, NY)
        return field / diag_a + back

    def apply_a(field):
        return operate(field, self_term, coef_x, coef_up, coef_y, coef_left)
    solution_field = jnp.zeros_like(right_side)
    residual = right_side
    pre = precondition(residual)
    direction = pre
    rz_now = jnp.sum(residual * pre)
    for step in range(ITERS):
        image = apply_a(direction)
        alpha = rz_now / jnp.sum(direction * image)
        solution_field = solution_field + alpha * direction
        residual = residual - alpha * image
        if step + 1 < ITERS:
            pre = precondition(residual)
            rz_next = jnp.sum(residual * pre)
            direction = pre + rz_next / rz_now * direction
            rz_now = rz_next
    return (solution_field, residual)
```

```python
import functools

import jax
import jax.numpy as jnp
from jax import lax
from jax.experimental import pallas as pl
from jax.experimental.pallas import tpu as pltpu
from jax.sharding import PartitionSpec as P

HIGH = lax.Precision.HIGHEST
MESH = pl.DeviceIdType.MESH
VMEM = pltpu.VMEM
SIDE = 4
B = 128
W = 8
TILES = B // W


def along_gx(index):
    return {"gx": index}


def gather_kernel(own_ref, whole, local_sem, send_sem, near_sem, far_sem, core_sem, core_send):
    rows = own_ref.shape[0]
    half = rows // 2
    me = lax.axis_index("gx")
    core = lax.rem(me, 2)
    y = lax.rem(me // 2, SIDE)
    x = me // (2 * SIDE)

    def at(a, b):
        xx = lax.rem(x + core * a + (1 - core) * b + 2 * SIDE, SIDE)
        yy = lax.rem(y + (1 - core) * a + core * b + 2 * SIDE, SIDE)
        return (xx * SIDE + yy) * 2 + core

    other = me + 1 - 2 * core
    peers = [at(1, 0), at(-1, 0), at(0, 1), at(0, -1), other]
    barrier = pltpu.get_barrier_semaphore()
    for peer in peers:
        pl.semaphore_signal(barrier, inc=1, device_id=along_gx(peer), device_id_type=MESH)
    pl.semaphore_wait(barrier, len(peers))

    def block(a, b, part=None):
        start = at(a, b) * rows
        if part is None:
            return whole.at[pl.ds(pl.multiple_of(start, rows), rows), :]
        return whole.at[pl.ds(pl.multiple_of(start + part * half, half), half), :]

    sent = []

    def send(a, b, part, peer, sem):
        source = own_ref if (a, b) == (0, 0) else block(a, b, part)
        copy = pltpu.make_async_remote_copy(
            src_ref=source,
            dst_ref=block(a, b, part),
            send_sem=send_sem.at[len(sent)],
            recv_sem=sem,
            device_id=along_gx(peer),
            device_id_type=MESH,
        )
        copy.start()
        sent.append(copy)

    crossed = []

    def cross(a, b):
        source = own_ref if (a, b) == (0, 0) else block(a, b)
        i = len(crossed)
        copy = pltpu.make_async_remote_copy(
            src_ref=source,
            dst_ref=block(a, b),
            send_sem=core_send.at[i],
            recv_sem=core_sem.at[i],
            device_id=along_gx(other),
            device_id_type=MESH,
        )
        copy.start()
        crossed.append(copy)

    def arrived(a, b, part, sem):
        ref = block(a, b, part)
        pltpu.make_async_copy(ref, ref, sem).wait()

    def spread(a):
        send(a, 0, None, peers[2], far_sem.at[a % SIDE, 0])
        send(a, 0, None, peers[3], far_sem.at[a % SIDE, 1])

    def spread_on(a):
        arrived(a, -1, None, far_sem.at[a % SIDE, 0])
        send(a, -1, 0, peers[2], far_sem.at[a % SIDE, 2])
        arrived(a, 1, None, far_sem.at[a % SIDE, 1])
        send(a, 1, 1, peers[3], far_sem.at[a % SIDE, 3])
        cross(a, -1)
        cross(a, 1)

    def spread_end(a):
        arrived(a, 2, 0, far_sem.at[a % SIDE, 2])
        arrived(a, 2, 1, far_sem.at[a % SIDE, 3])
        cross(a, 2)

    send(0, 0, None, peers[0], near_sem.at[0])
    send(0, 0, None, peers[1], near_sem.at[1])
    spread(0)
    cross(0, 0)
    mine = pltpu.make_async_copy(own_ref, block(0, 0), local_sem)
    mine.start()
    arrived(-1, 0, None, near_sem.at[0])
    send(-1, 0, 0, peers[0], near_sem.at[2])
    spread(-1)
    arrived(1, 0, None, near_sem.at[1])
    send(1, 0, 1, peers[1], near_sem.at[3])
    spread(1)
    cross(-1, 0)
    cross(1, 0)
    spread_on(0)
    arrived(2, 0, 0, near_sem.at[2])
    arrived(2, 0, 1, near_sem.at[3])
    spread(2)
    cross(2, 0)
    spread_on(-1)
    spread_end(0)
    spread_on(1)
    spread_end(-1)
    spread_on(2)
    spread_end(1)
    spread_end(2)
    mine.wait()
    for copy in sent:
        copy.wait_send()
    for copy in crossed:
        copy.wait()


def gather(own):
    rows, columns = own.shape
    return pl.pallas_call(
        gather_kernel,
        out_shape=jax.ShapeDtypeStruct((32 * rows, columns), own.dtype),
        in_specs=[pl.BlockSpec(memory_space=VMEM)],
        out_specs=pl.BlockSpec(memory_space=pl.ANY),
        scratch_shapes=[
            pltpu.SemaphoreType.DMA,
            pltpu.SemaphoreType.DMA((20,)),
            pltpu.SemaphoreType.DMA((4,)),
            pltpu.SemaphoreType.DMA((4, 4)),
            pltpu.SemaphoreType.DMA((16,)),
            pltpu.SemaphoreType.DMA((16,)),
        ],
        compiler_params=pltpu.CompilerParams(collective_id=0, has_side_effects=True),
        name="gather",
    )(own)


def dot(a, b, contract=(1, 0)):
    dims = (((contract[0],), (contract[1],)), ((), ()))
    return lax.dot_general(a, b, dims, precision=HIGH, preferred_element_type=jnp.float32)


def invert_block(load):
    sub = lax.broadcasted_iota(jnp.int32, (W, B), 0)
    lane = lax.broadcasted_iota(jnp.int32, (W, B), 1)
    a = [load(i) for i in range(TILES)]

    def row(t, j):
        return jnp.broadcast_to(t[j : j + 1, :], (W, B))

    def column(t, j):
        return jnp.broadcast_to(t[:, j : j + 1], (W, B))

    for p in range(TILES):
        t = a[p]
        cols = [[column(a[i], p * W + j) for j in range(W)] for i in range(TILES)]
        b = list(cols[p])
        for j in range(W):
            r = 1.0 / row(b[j], j)
            m = b[j] * r
            t = jnp.where(lane == p * W + j, jnp.where(sub == j, 1.0, 0.0), t)
            tj = row(t, j)
            t = jnp.where(sub == j, tj * r, t - m * tj)
            for q in range(j + 1, W):
                bj = row(b[q], j)
                b[q] = jnp.where(sub == j, bj * r, b[q] - m * bj)
        rows = [row(t, j) for j in range(W)]
        keep = (lane < p * W) | (lane >= (p + 1) * W)
        for i in [(p + 1 + s) % TILES for s in range(TILES - 1)]:
            s = [cols[i][2 * h] * rows[2 * h] + cols[i][2 * h + 1] * rows[2 * h + 1] for h in range(W // 2)]
            a[i] = jnp.where(keep, a[i], 0.0) - ((s[0] + s[1]) + (s[2] + s[3]))
        a[p] = t
    return a


def inverse_kernel(e_ref, t_ref, e, unit, pivots):
    own, size = t_ref.shape
    blocks = size // B
    e[...] = e_ref[...]
    first = lax.axis_index("gx") * own
    at = lax.broadcasted_iota(jnp.int32, (own, size), 1) - lax.broadcasted_iota(jnp.int32, (own, size), 0)
    unit[...] = jnp.where(at == first, 1.0, 0.0)
    for k in range(blocks):
        o = k * B
        for i, tile in enumerate(invert_block(lambda i: e[o + i * W : o + (i + 1) * W, o : o + B])):
            pivots[k, i * W : (i + 1) * W, :] = tile
        if k + 1 < blocks:
            panel = dot(pivots[k], e[o : o + B, o + B :])
            unit[:, o + B :] -= dot(unit[:, o : o + B], panel)
            e[o + B :, o + B :] -= dot(e[o : o + B, o + B :], panel, (0, 0))
    for k in reversed(range(blocks)):
        o = k * B
        x = unit[:, o : o + B]
        if k + 1 < blocks:
            x = x - dot(t_ref[:, o + B :], e[o : o + B, o + B :], (1, 1))
        t_ref[:, o : o + B] = dot(x, pivots[k])


def inverse_rows(whole, own):
    size = whole.shape[0]
    return pl.pallas_call(
        inverse_kernel,
        out_shape=jax.ShapeDtypeStruct((own, size), jnp.float32),
        in_specs=[pl.BlockSpec(memory_space=VMEM)],
        out_specs=pl.BlockSpec(memory_space=VMEM),
        scratch_shapes=[
            VMEM((size, size), jnp.float32),
            VMEM((own, size), jnp.float32),
            VMEM((size // B, B, B), jnp.float32),
        ],
        compiler_params=pltpu.CompilerParams(vmem_limit_bytes=48 * 2**20),
        name="inverse_rows",
    )(whole)


def total(a):
    return jnp.sum(jnp.sum(a, axis=0, keepdims=True), axis=1, keepdims=True)


def cg_kernel(
    n_gx, n_gy, rhs_ref, shift_ref, fx_ref, fy_ref, mask_ref, v_ref, t_ref, x_ref, res_ref,
    u0_ref, w0_ref, z1_ref, s1_ref, cu_ref, cl_ref, diag_ref, y_ref,
    msg, coef, sums, group, line, edge_out, edge_in, face_out, face_in,
    coef_send, coef_recv, group_send, group_recv, line_send, line_recv, edge_send, edge_recv, face_send, face_recv,
):
    vectors, cx_n, cy_n = v_ref.shape
    gx, gy = lax.axis_index("gx"), lax.axis_index("gy")
    lane1 = lax.broadcasted_iota(jnp.int32, (1, cy_n), 1)
    row2 = lax.broadcasted_iota(jnp.int32, (cx_n, cy_n), 0)
    lane2 = lax.broadcasted_iota(jnp.int32, (cx_n, cy_n), 1)
    eye = row2 == lane2

    def along(axis, count, step):
        return {axis: lax.rem(lax.axis_index(axis) + step, count)}

    below, above = along("gx", n_gx, 1), along("gx", n_gx, n_gx - 1)
    right, left = along("gy", n_gy, 1), along("gy", n_gy, n_gy - 1)

    barrier = pltpu.get_barrier_semaphore()
    for axis, count in (("gx", n_gx), ("gy", n_gy)):

        def greet(step, carry, axis=axis, count=count):
            pl.semaphore_signal(barrier, inc=1, device_id=along(axis, count, step), device_id_type=MESH)
            return carry

        lax.fori_loop(1, count, greet, 0)

    mask = mask_ref[...].astype(jnp.float32)
    cx = fx_ref[...] * mask
    cy = fy_ref[...] * mask
    self_term = shift_ref[...] * mask + (1.0 - mask)

    def as_row(column):
        return jnp.sum(jnp.where(eye, column, 0.0), axis=0, keepdims=True)

    def as_column(row):
        return jnp.sum(jnp.where(eye, row, 0.0), axis=1, keepdims=True)

    face_out[0] = cx[cx_n - 1 :, :]
    face_out[1] = as_row(cy[:, cy_n - 1 :])

    def coefficients(field):
        parts = jnp.sum(v_ref[...] * field[None], axis=1)
        column = jnp.sum(parts, axis=1, keepdims=True)
        place = lax.rem(gx, cy_n // vectors) * vectors + lax.broadcasted_iota(jnp.int32, (vectors, cy_n), 0)
        here = lax.broadcasted_iota(jnp.int32, (vectors, cy_n), 1) == place
        return jnp.sum(jnp.where(here, column, 0.0), axis=0, keepdims=True)

    first = coefficients(rhs_ref[...])

    pl.semaphore_wait(barrier, n_gx + n_gy - 2)

    faces = []
    for i, (peer, name) in enumerate(((below, "x"), (right, "y"))):
        copy = pltpu.make_async_remote_copy(
            src_ref=face_out.at[i], dst_ref=face_in.at[i], send_sem=face_send.at[i], recv_sem=face_recv.at[i],
            device_id=peer, device_id_type=MESH,
        )
        copy.start()
        faces.append(copy)

    def share(source, slots, axis, count, send, recv):
        me = lax.axis_index(axis)
        slots[me] = source[...]

        def one(step, carry):
            pltpu.make_async_remote_copy(
                src_ref=source, dst_ref=slots.at[me], send_sem=send, recv_sem=recv,
                device_id=along(axis, count, step), device_id_type=MESH,
            ).start()
            return carry

        lax.fori_loop(1, count, one, 0)

    def shared(slots, count, send, recv):
        others = slots.at[pl.ds(0, count - 1)]
        pltpu.make_async_copy(others, others, recv).wait()
        pltpu.make_async_copy(others, others, send).wait()

    def send_coefficients(i, row):
        msg[i] = row
        share(msg.at[i], coef.at[i], "gx", n_gx, coef_send.at[i], coef_recv.at[i])

    def gathered(i):
        shared(coef.at[i], n_gx, coef_send.at[i], coef_recv.at[i])
        each = cy_n // vectors
        return [sum(coef[i, p * each + j] for j in range(1, each)) + coef[i, p * each] for p in range(n_gx // each)]

    def expand(rows):
        acc = sum(t_ref[:, p * cy_n : (p + 1) * cy_n] * row for p, row in enumerate(rows))
        y_ref[...] = jnp.broadcast_to(jnp.sum(acc, axis=1, keepdims=True), (vectors, cy_n))
        out = v_ref[0] * y_ref[0:1, :]
        for k in range(1, vectors):
            out = out + v_ref[k] * y_ref[k : k + 1, :]
        return out

    def apply(i, field):
        edge_out[i, 0] = field[cx_n - 1 :, :]
        edge_out[i, 1] = field[0:1, :]
        edge_out[i, 2] = as_row(field[:, cy_n - 1 :])
        edge_out[i, 3] = as_row(field[:, 0:1])
        copies = []
        for j, peer in enumerate((below, above, right, left)):
            copy = pltpu.make_async_remote_copy(
                src_ref=edge_out.at[i, j], dst_ref=edge_in.at[i, j],
                send_sem=edge_send.at[i, j], recv_sem=edge_recv.at[i, j],
                device_id=peer, device_id_type=MESH,
            )
            copy.start()
            copies.append(copy)
        down = pltpu.roll(field, cx_n - 1, 0)
        up = pltpu.roll(field, 1, 0)
        to_right = pltpu.roll(field, cy_n - 1, 1)
        to_left = pltpu.roll(field, 1, 1)
        for copy in copies:
            copy.wait()
        zero = jnp.zeros((1, cy_n), jnp.float32)
        from_above = jnp.where(gx > 0, edge_in[i, 0], zero)
        from_below = jnp.where(gx < n_gx - 1, edge_in[i, 1], zero)
        from_left = jnp.where(gy > 0, edge_in[i, 2], zero)
        from_right = jnp.where(gy < n_gy - 1, edge_in[i, 3], zero)
        down = jnp.where(row2 == cx_n - 1, from_below, down)
        up = jnp.where(row2 == 0, from_above, up)
        to_right = jnp.where(lane2 == cy_n - 1, as_column(from_right), to_right)
        to_left = jnp.where(lane2 == 0, as_column(from_left), to_left)
        mask = mask_ref[...].astype(jnp.float32)
        self_term = shift_ref[...] * mask + (1.0 - mask)
        return (
            self_term * field
            + fx_ref[...] * mask * (field - down)
            + cu_ref[...] * (field - up)
            + fy_ref[...] * mask * (field - to_right)
            + cl_ref[...] * (field - to_left)
        )

    def packed(values):
        row = jnp.zeros((1, cy_n), jnp.float32)
        for i, value in enumerate(values):
            row = jnp.where(lane1 == i, value, row)
        return row

    def sum_over_group(i, values):
        sums[i, 0] = packed(values)
        share(sums.at[i, 0], group.at[i], "gx", n_gx, group_send.at[i], group_recv.at[i])

    def sum_over_lines(i):
        shared(group.at[i], n_gx, group_send.at[i], group_recv.at[i])
        sums[i, 1] = sum(group[i, d] for d in range(1, n_gx)) + group[i, 0]
        share(sums.at[i, 1], line.at[i], "gy", n_gy, line_send.at[i], line_recv.at[i])

    def summed(i):
        shared(line.at[i], n_gy, line_send.at[i], line_recv.at[i])
        row = sum(line[i, d] for d in range(1, n_gy)) + line[i, 0]

        def value(j):
            return jnp.sum(jnp.where(lane1 == j, row, 0.0), axis=1, keepdims=True)

        return value

    send_coefficients(0, first)
    for copy in faces:
        copy.wait()
    upper = jnp.where(gx > 0, face_in[0], jnp.zeros((1, cy_n), jnp.float32))
    beside = jnp.where(gy > 0, face_in[1], jnp.zeros((1, cy_n), jnp.float32))
    cu = jnp.where(row2 == 0, upper, pltpu.roll(cx, 1, 0))
    cl = jnp.where(lane2 == 0, as_column(beside), pltpu.roll(cy, 1, 1))
    cu_ref[...] = cu
    cl_ref[...] = cl
    inverse_diag = 1.0 / (self_term + cx + cu + cy + cl)
    diag_ref[...] = inverse_diag
    u0 = rhs_ref[...] * inverse_diag + expand(gathered(0))
    u0_ref[...] = u0
    w0 = apply(0, u0)
    w0_ref[...] = w0

    send_coefficients(1, coefficients(w0))
    sum_over_group(0, [total(rhs_ref[...] * u0), total(u0 * w0)])
    rows_w0 = gathered(1)
    u1 = w0_ref[...] * diag_ref[...] + expand(rows_w0)
    sum_over_lines(0)
    w1 = apply(1, u1)

    send_coefficients(2, coefficients(w1))
    rows_w1 = gathered(2)
    value = summed(0)
    g00 = value(1)
    alpha0 = value(0) / g00
    z1 = u0_ref[...] - alpha0 * u1
    s1 = w0_ref[...] - alpha0 * w1
    z1_ref[...] = z1
    s1_ref[...] = s1
    q = alpha0 * s1 * diag_ref[...] + expand([alpha0 * (a - alpha0 * b) for a, b in zip(rows_w0, rows_w1)])
    v = apply(2, q)

    r1 = rhs_ref[...] - alpha0 * w0_ref[...]
    u0, z1, s1 = u0_ref[...], z1_ref[...], s1_ref[...]
    sum_over_group(1, [total(u0 * s1), total(u0 * v), total(z1 * s1), total(z1 * v), total(q * v), total(z1 * r1), total(q * r1)])
    sum_over_lines(1)
    value = summed(1)
    g01, g02, g11, g12, g22, b1, b2 = [value(j) for j in range(7)]
    l10 = g01 / g00
    l20 = g02 / g00
    d1 = g11 - l10 * g01
    e12 = g12 - l20 * g01
    l21 = e12 / d1
    d2 = g22 - l20 * g02 - l21 * e12
    c2 = (b2 - l21 * b1) / d2
    c1 = b1 / d1 - l21 * c2
    c0 = -(l10 * c1 + l20 * c2)
    x_ref[...] = (alpha0 + c0) * u0 + c1 * z1 + c2 * q
    res_ref[...] = r1 - c0 * w0_ref[...] - c1 * s1 - c2 * v


def conjugate_gradients(n_gx, n_gy, *args):
    tile = args[0].shape
    vectors, _, lanes = args[5].shape
    field = VMEM(tile, jnp.float32)
    dma = pltpu.SemaphoreType.DMA
    f32 = jnp.float32
    return pl.pallas_call(
        functools.partial(cg_kernel, n_gx, n_gy),
        out_shape=(jax.ShapeDtypeStruct(tile, f32),) * 2,
        in_specs=[pl.BlockSpec(memory_space=VMEM)] * 7,
        out_specs=(pl.BlockSpec(memory_space=VMEM),) * 2,
        scratch_shapes=[field] * 7
        + [
            VMEM((vectors, lanes), f32),
            VMEM((3, 1, lanes), f32),
            VMEM((3, n_gx, 1, lanes), f32),
            VMEM((2, 2, 1, lanes), f32),
            VMEM((2, n_gx, 1, lanes), f32),
            VMEM((2, n_gy, 1, lanes), f32),
            VMEM((3, 4, 1, lanes), f32),
            VMEM((3, 4, 1, lanes), f32),
            VMEM((2, 1, lanes), f32),
            VMEM((2, 1, lanes), f32),
            dma((3,)), dma((3,)), dma((2,)), dma((2,)), dma((2,)), dma((2,)),
            dma((3, 4)), dma((3, 4)), dma((2,)), dma((2,)),
        ],
        compiler_params=pltpu.CompilerParams(collective_id=1, has_side_effects=True, vmem_limit_bytes=32 * 2**20),
        name="conjugate_gradients",
    )(*args)


def body(n_gx, n_gy, right_side, shift, face_x, face_y, ice_mask, deflation, coarse_matrix):
    whole = gather(coarse_matrix[0])
    rows = inverse_rows(whole, coarse_matrix.shape[1])
    return conjugate_gradients(n_gx, n_gy, right_side, shift, face_x, face_y, ice_mask, deflation, rows)


def solution(mesh):
    in_specs = (
        P("gx", "gy"),
        P("gx", "gy"),
        P("gx", "gy"),
        P("gx", "gy"),
        P("gx", "gy"),
        P(None, "gx", "gy"),
        P("gy", "gx", None),
    )
    out_specs = (P("gx", "gy"), P("gx", "gy"))
    run = functools.partial(body, mesh.shape["gx"], mesh.shape["gy"])
    return jax.shard_map(run, mesh=mesh, in_specs=in_specs, out_specs=out_specs, check_vma=False)
```

```python
import functools

import jax
import jax.numpy as jnp
from jax import lax
from jax.experimental import pallas as pl
from jax.experimental.pallas import tpu as pltpu
from jax.sharding import PartitionSpec as P

HIGH = lax.Precision.HIGHEST
MESH = pl.DeviceIdType.MESH
VMEM = pltpu.VMEM
SIDE = 4
B = 128
W = 8
TILES = B // W
GROUP = 4


def along_gx(index):
    return {"gx": index}


def gather_kernel(own_ref, whole, local_sem, send_sem, near_sem, far_sem, core_sem, core_send):
    rows = own_ref.shape[0]
    half = rows // 2
    me = lax.axis_index("gx")
    core = lax.rem(me, 2)
    y = lax.rem(me // 2, SIDE)
    x = me // (2 * SIDE)

    def at(a, b):
        xx = lax.rem(x + core * a + (1 - core) * b + 2 * SIDE, SIDE)
        yy = lax.rem(y + (1 - core) * a + core * b + 2 * SIDE, SIDE)
        return (xx * SIDE + yy) * 2 + core

    other = me + 1 - 2 * core
    peers = [at(1, 0), at(-1, 0), at(0, 1), at(0, -1), other]
    barrier = pltpu.get_barrier_semaphore()
    for peer in peers:
        pl.semaphore_signal(barrier, inc=1, device_id=along_gx(peer), device_id_type=MESH)
    pl.semaphore_wait(barrier, len(peers))

    def block(a, b, part=None):
        start = at(a, b) * rows
        if part is None:
            return whole.at[pl.ds(pl.multiple_of(start, rows), rows), :]
        return whole.at[pl.ds(pl.multiple_of(start + part * half, half), half), :]

    sent = []

    def send(a, b, part, peer, sem):
        source = own_ref if (a, b) == (0, 0) else block(a, b, part)
        copy = pltpu.make_async_remote_copy(
            src_ref=source,
            dst_ref=block(a, b, part),
            send_sem=send_sem.at[len(sent)],
            recv_sem=sem,
            device_id=along_gx(peer),
            device_id_type=MESH,
        )
        copy.start()
        sent.append(copy)

    crossed = []

    def cross(a, b):
        source = own_ref if (a, b) == (0, 0) else block(a, b)
        i = len(crossed)
        copy = pltpu.make_async_remote_copy(
            src_ref=source,
            dst_ref=block(a, b),
            send_sem=core_send.at[i],
            recv_sem=core_sem.at[i],
            device_id=along_gx(other),
            device_id_type=MESH,
        )
        copy.start()
        crossed.append(copy)

    def arrived(a, b, part, sem):
        ref = block(a, b, part)
        pltpu.make_async_copy(ref, ref, sem).wait()

    def spread(a):
        send(a, 0, None, peers[2], far_sem.at[a % SIDE, 0])
        send(a, 0, None, peers[3], far_sem.at[a % SIDE, 1])

    def spread_on(a):
        arrived(a, -1, None, far_sem.at[a % SIDE, 0])
        send(a, -1, 0, peers[2], far_sem.at[a % SIDE, 2])
        arrived(a, 1, None, far_sem.at[a % SIDE, 1])
        send(a, 1, 1, peers[3], far_sem.at[a % SIDE, 3])
        cross(a, -1)
        cross(a, 1)

    def spread_end(a):
        arrived(a, 2, 0, far_sem.at[a % SIDE, 2])
        arrived(a, 2, 1, far_sem.at[a % SIDE, 3])
        cross(a, 2)

    send(0, 0, None, peers[0], near_sem.at[0])
    send(0, 0, None, peers[1], near_sem.at[1])
    spread(0)
    cross(0, 0)
    mine = pltpu.make_async_copy(own_ref, block(0, 0), local_sem)
    mine.start()
    arrived(-1, 0, None, near_sem.at[0])
    send(-1, 0, 0, peers[0], near_sem.at[2])
    spread(-1)
    arrived(1, 0, None, near_sem.at[1])
    send(1, 0, 1, peers[1], near_sem.at[3])
    spread(1)
    cross(-1, 0)
    cross(1, 0)
    spread_on(0)
    arrived(2, 0, 0, near_sem.at[2])
    arrived(2, 0, 1, near_sem.at[3])
    spread(2)
    cross(2, 0)
    spread_on(-1)
    spread_end(0)
    spread_on(1)
    spread_end(-1)
    spread_on(2)
    spread_end(1)
    spread_end(2)
    mine.wait()
    for copy in sent:
        copy.wait_send()
    for copy in crossed:
        copy.wait()


def gather(own):
    rows, columns = own.shape
    return pl.pallas_call(
        gather_kernel,
        out_shape=jax.ShapeDtypeStruct((32 * rows, columns), own.dtype),
        in_specs=[pl.BlockSpec(memory_space=VMEM)],
        out_specs=pl.BlockSpec(memory_space=pl.ANY),
        scratch_shapes=[
            pltpu.SemaphoreType.DMA,
            pltpu.SemaphoreType.DMA((20,)),
            pltpu.SemaphoreType.DMA((4,)),
            pltpu.SemaphoreType.DMA((4, 4)),
            pltpu.SemaphoreType.DMA((16,)),
            pltpu.SemaphoreType.DMA((16,)),
        ],
        compiler_params=pltpu.CompilerParams(collective_id=0, has_side_effects=True),
        name="gather",
    )(own)


def dot(a, b, contract=(1, 0)):
    dims = (((contract[0],), (contract[1],)), ((), ()))
    return lax.dot_general(a, b, dims, precision=HIGH, preferred_element_type=jnp.float32)


def invert_block(load, ones, between):
    sub = lax.broadcasted_iota(jnp.int32, (W, B), 0)
    lane = lax.broadcasted_iota(jnp.int32, (W, B), 1)
    zero = jnp.zeros((W, B), jnp.float32)
    a = [load(i) for i in range(TILES)]
    low, scaled = [], []

    def row(t, j):
        return jnp.broadcast_to(t[j : j + 1, :], (W, B))

    def column(t, j):
        return jnp.broadcast_to(t[:, j : j + 1], (W, B))

    for g in range(0, TILES, GROUP):
        pair = range(g, g + GROUP)
        for i in pair:
            low.append(jnp.where(lane < g * W, a[i], jnp.where(lane == i * W + sub, 1.0, 0.0)))
        for p in pair:
            t = a[p]
            own = (lane >= p * W) & (lane < (p + 1) * W)
            others = [i for i in pair if i != p]
            b = [column(t, p * W + j) * ones for j in range(W)]
            c = {(i, j): column(a[i], p * W + j) for i in others for j in range(W)}
            t = jnp.where(own, jnp.where(lane == p * W + sub, 1.0, 0.0), t)
            for j in range(0, W, 2):
                k = j + 1
                first, both, second = row(b[j], j), row(b[k], j), row(b[k], k)
                f = 1.0 / (first * second - both * both)
                two = (sub == j) | (sub == k)
                m, n = jnp.where(two, 0.0, b[j]), jnp.where(two, 0.0, b[k])

                def eliminate(v):
                    vj, vk = row(v, j), row(v, k)
                    nj = (second * vj - both * vk) * f
                    nk = (first * vk - both * vj) * f
                    return jnp.where(sub == j, nj, jnp.where(sub == k, nk, v - (m * nj + n * nk)))

                b = [eliminate(b[q]) if q > k else None for q in range(W)]
                t = eliminate(t)
            rows = [row(t, j) for j in range(W)]
            for i in others:
                s = [c[i, 2 * h] * rows[2 * h] + c[i, 2 * h + 1] * rows[2 * h + 1] for h in range(W // 2)]
                a[i] = jnp.where(own, 0.0, a[i]) - ((s[0] + s[1]) + (s[2] + s[3]))
            a[p] = t
        end = (g + GROUP) * W
        scaled += [jnp.where(lane < end, a[i], 0.0) for i in pair]
        if g + GROUP < TILES:
            inside = (lane >= g * W) & (lane < end)
            weights = [zero] * g + [a[i] for i in pair] + [zero] * (TILES - g - GROUP)
            change = dot(jnp.concatenate(a[g + GROUP :], 0), jnp.concatenate(weights, 0))
            for n, i in enumerate(range(g + GROUP, TILES)):
                a[i] = jnp.where(inside, 0.0, a[i]) - change[n * W : (n + 1) * W]
        between(g // GROUP)
    return dot(jnp.concatenate(low, 0), jnp.concatenate(scaled, 0), (0, 0))


def inverse_kernel(e_ref, t_ref, e, panels, unit, scale):
    own, size = t_ref.shape
    blocks = size // B
    first = lax.axis_index("gx") * own
    at = lax.broadcasted_iota(jnp.int32, (own, size), 1) - lax.broadcasted_iota(jnp.int32, (own, size), 0)
    eye = lax.broadcasted_iota(jnp.int32, (B, B), 0) == lax.broadcasted_iota(jnp.int32, (B, B), 1)
    waiting = []

    def between(i):
        left = TILES // GROUP - 1 - i
        count = len(waiting) if left == 0 else -(-len(waiting) // (left + 1))
        for _ in range(count):
            waiting.pop(0)()

    def span(k):
        return slice(k * B, (k + 1) * B)

    by_row = []
    for k in range(blocks):
        diagonal = jnp.where(eye, e_ref[span(k), span(k)], 0.0)
        scale[:, span(k)] = lax.rsqrt(jnp.sum(diagonal, axis=0, keepdims=True))
        by_row.append(lax.rsqrt(jnp.sum(diagonal, axis=1, keepdims=True)))
    for k in range(blocks):
        upper = slice(k * B, size)
        e[span(k), upper] = e_ref[span(k), upper] * by_row[k] * scale[:, upper]
    unit[...] = jnp.where(at == first, scale[...], 0.0)
    ones = jnp.broadcast_to(jnp.minimum(scale[:, :B] + 1.0, 1.0), (W, B))

    def trail(k, i, columns):
        e[span(i), columns] -= dot(e[span(k), span(i)], panels[span(k), columns], (0, 0))

    for k in range(blocks):
        d = invert_block(lambda i: e[k * B + i * W : k * B + (i + 1) * W, span(k)], ones, between)
        if k + 1 < blocks:
            after = slice((k + 1) * B, size)
            panels[span(k), span(k + 1)] = dot(d, e[span(k), span(k + 1)])
            trail(k, k + 1, span(k + 1))

            def rest(k=k, d=d):
                far = slice((k + 2) * B, size)
                panels[span(k), far] = dot(d, e[span(k), far])

            def across(k=k, after=after):
                unit[:, after] -= dot(unit[:, span(k)], panels[span(k), after])

            if k + 2 < blocks:
                waiting.append(rest)
                for i in range(k + 1, blocks):
                    for j in range(max(i, k + 2), blocks, 2):
                        columns = slice(j * B, min(j + 2, blocks) * B)
                        waiting.append(lambda k=k, i=i, columns=columns: trail(k, i, columns))
            waiting.append(across)
        waiting.append(lambda k=k, d=d: t_ref.__setitem__((slice(None), span(k)), dot(unit[:, span(k)], d)))
    for work in waiting:
        work()
    for k in reversed(range(blocks - 1)):
        after = slice((k + 1) * B, size)
        t_ref[:, span(k)] -= dot(t_ref[:, after], panels[span(k), after], (1, 1))
    t_ref[...] *= scale[...]


def inverse_rows(whole, own):
    size = whole.shape[0]
    return pl.pallas_call(
        inverse_kernel,
        out_shape=jax.ShapeDtypeStruct((own, size), jnp.float32),
        in_specs=[pl.BlockSpec(memory_space=VMEM)],
        out_specs=pl.BlockSpec(memory_space=VMEM),
        scratch_shapes=[
            VMEM((size, size), jnp.float32),
            VMEM((size, size), jnp.float32),
            VMEM((own, size), jnp.float32),
            VMEM((1, size), jnp.float32),
        ],
        compiler_params=pltpu.CompilerParams(vmem_limit_bytes=48 * 2**20),
        name="inverse_rows",
    )(whole)


def total(a):
    return jnp.sum(jnp.sum(a, axis=0, keepdims=True), axis=1, keepdims=True)


def cg_kernel(
    n_gx, n_gy, rhs_ref, shift_ref, fx_ref, fy_ref, mask_ref, v_ref, t_ref, x_ref, res_ref,
    u0_ref, w0_ref, z1_ref, s1_ref, cu_ref, cl_ref, diag_ref, y_ref,
    msg, coef, sums, group, line, edge_out, edge_in, face_out, face_in,
    coef_send, coef_recv, group_send, group_recv, line_send, line_recv, edge_send, edge_recv, face_send, face_recv,
):
    vectors, cx_n, cy_n = v_ref.shape
    gx, gy = lax.axis_index("gx"), lax.axis_index("gy")
    lane1 = lax.broadcasted_iota(jnp.int32, (1, cy_n), 1)
    row2 = lax.broadcasted_iota(jnp.int32, (cx_n, cy_n), 0)
    lane2 = lax.broadcasted_iota(jnp.int32, (cx_n, cy_n), 1)
    eye = row2 == lane2

    def along(axis, count, step):
        return {axis: lax.rem(lax.axis_index(axis) + step, count)}

    below, above = along("gx", n_gx, 1), along("gx", n_gx, n_gx - 1)
    right, left = along("gy", n_gy, 1), along("gy", n_gy, n_gy - 1)

    barrier = pltpu.get_barrier_semaphore()
    for axis, count in (("gx", n_gx), ("gy", n_gy)):

        def greet(step, carry, axis=axis, count=count):
            pl.semaphore_signal(barrier, inc=1, device_id=along(axis, count, step), device_id_type=MESH)
            return carry

        lax.fori_loop(1, count, greet, 0)

    mask = mask_ref[...].astype(jnp.float32)
    cx = fx_ref[...] * mask
    cy = fy_ref[...] * mask
    self_term = shift_ref[...] * mask + (1.0 - mask)

    def as_row(column):
        return jnp.sum(jnp.where(eye, column, 0.0), axis=0, keepdims=True)

    def as_column(row):
        return jnp.sum(jnp.where(eye, row, 0.0), axis=1, keepdims=True)

    face_out[0] = cx[cx_n - 1 :, :]
    face_out[1] = as_row(cy[:, cy_n - 1 :])

    def coefficients(field):
        parts = jnp.sum(v_ref[...] * field[None], axis=1)
        column = jnp.sum(parts, axis=1, keepdims=True)
        place = lax.rem(gx, cy_n // vectors) * vectors + lax.broadcasted_iota(jnp.int32, (vectors, cy_n), 0)
        here = lax.broadcasted_iota(jnp.int32, (vectors, cy_n), 1) == place
        return jnp.sum(jnp.where(here, column, 0.0), axis=0, keepdims=True)

    first = coefficients(rhs_ref[...])

    pl.semaphore_wait(barrier, n_gx + n_gy - 2)

    faces = []
    for i, (peer, name) in enumerate(((below, "x"), (right, "y"))):
        copy = pltpu.make_async_remote_copy(
            src_ref=face_out.at[i], dst_ref=face_in.at[i], send_sem=face_send.at[i], recv_sem=face_recv.at[i],
            device_id=peer, device_id_type=MESH,
        )
        copy.start()
        faces.append(copy)

    def share(source, slots, axis, count, send, recv):
        me = lax.axis_index(axis)
        slots[me] = source[...]

        def one(step, carry):
            pltpu.make_async_remote_copy(
                src_ref=source, dst_ref=slots.at[me], send_sem=send, recv_sem=recv,
                device_id=along(axis, count, step), device_id_type=MESH,
            ).start()
            return carry

        lax.fori_loop(1, count, one, 0)

    def shared(slots, count, send, recv):
        others = slots.at[pl.ds(0, count - 1)]
        pltpu.make_async_copy(others, others, recv).wait()
        pltpu.make_async_copy(others, others, send).wait()

    def send_coefficients(i, row):
        msg[i] = row
        share(msg.at[i], coef.at[i], "gx", n_gx, coef_send.at[i], coef_recv.at[i])

    def gathered(i):
        shared(coef.at[i], n_gx, coef_send.at[i], coef_recv.at[i])
        each = cy_n // vectors
        return [sum(coef[i, p * each + j] for j in range(1, each)) + coef[i, p * each] for p in range(n_gx // each)]

    def expand(rows):
        acc = sum(t_ref[:, p * cy_n : (p + 1) * cy_n] * row for p, row in enumerate(rows))
        y_ref[...] = jnp.broadcast_to(jnp.sum(acc, axis=1, keepdims=True), (vectors, cy_n))
        out = v_ref[0] * y_ref[0:1, :]
        for k in range(1, vectors):
            out = out + v_ref[k] * y_ref[k : k + 1, :]
        return out

    def apply(i, field):
        edge_out[i, 0] = field[cx_n - 1 :, :]
        edge_out[i, 1] = field[0:1, :]
        edge_out[i, 2] = as_row(field[:, cy_n - 1 :])
        edge_out[i, 3] = as_row(field[:, 0:1])
        copies = []
        for j, peer in enumerate((below, above, right, left)):
            copy = pltpu.make_async_remote_copy(
                src_ref=edge_out.at[i, j], dst_ref=edge_in.at[i, j],
                send_sem=edge_send.at[i, j], recv_sem=edge_recv.at[i, j],
                device_id=peer, device_id_type=MESH,
            )
            copy.start()
            copies.append(copy)
        down = pltpu.roll(field, cx_n - 1, 0)
        up = pltpu.roll(field, 1, 0)
        to_right = pltpu.roll(field, cy_n - 1, 1)
        to_left = pltpu.roll(field, 1, 1)
        for copy in copies:
            copy.wait()
        zero = jnp.zeros((1, cy_n), jnp.float32)
        from_above = jnp.where(gx > 0, edge_in[i, 0], zero)
        from_below = jnp.where(gx < n_gx - 1, edge_in[i, 1], zero)
        from_left = jnp.where(gy > 0, edge_in[i, 2], zero)
        from_right = jnp.where(gy < n_gy - 1, edge_in[i, 3], zero)
        down = jnp.where(row2 == cx_n - 1, from_below, down)
        up = jnp.where(row2 == 0, from_above, up)
        to_right = jnp.where(lane2 == cy_n - 1, as_column(from_right), to_right)
        to_left = jnp.where(lane2 == 0, as_column(from_left), to_left)
        mask = mask_ref[...].astype(jnp.float32)
        self_term = shift_ref[...] * mask + (1.0 - mask)
        return (
            self_term * field
            + fx_ref[...] * mask * (field - down)
            + cu_ref[...] * (field - up)
            + fy_ref[...] * mask * (field - to_right)
            + cl_ref[...] * (field - to_left)
        )

    def packed(values):
        row = jnp.zeros((1, cy_n), jnp.float32)
        for i, value in enumerate(values):
            row = jnp.where(lane1 == i, value, row)
        return row

    def sum_over_group(i, values):
        sums[i, 0] = packed(values)
        share(sums.at[i, 0], group.at[i], "gx", n_gx, group_send.at[i], group_recv.at[i])

    def sum_over_lines(i):
        shared(group.at[i], n_gx, group_send.at[i], group_recv.at[i])
        sums[i, 1] = sum(group[i, d] for d in range(1, n_gx)) + group[i, 0]
        share(sums.at[i, 1], line.at[i], "gy", n_gy, line_send.at[i], line_recv.at[i])

    def summed(i):
        shared(line.at[i], n_gy, line_send.at[i], line_recv.at[i])
        row = sum(line[i, d] for d in range(1, n_gy)) + line[i, 0]

        def value(j):
            return jnp.sum(jnp.where(lane1 == j, row, 0.0), axis=1, keepdims=True)

        return value

    send_coefficients(0, first)
    for copy in faces:
        copy.wait()
    upper = jnp.where(gx > 0, face_in[0], jnp.zeros((1, cy_n), jnp.float32))
    beside = jnp.where(gy > 0, face_in[1], jnp.zeros((1, cy_n), jnp.float32))
    cu = jnp.where(row2 == 0, upper, pltpu.roll(cx, 1, 0))
    cl = jnp.where(lane2 == 0, as_column(beside), pltpu.roll(cy, 1, 1))
    cu_ref[...] = cu
    cl_ref[...] = cl
    inverse_diag = 1.0 / (self_term + cx + cu + cy + cl)
    diag_ref[...] = inverse_diag
    u0 = rhs_ref[...] * inverse_diag + expand(gathered(0))
    u0_ref[...] = u0
    w0 = apply(0, u0)
    w0_ref[...] = w0

    send_coefficients(1, coefficients(w0))
    sum_over_group(0, [total(rhs_ref[...] * u0), total(u0 * w0)])
    rows_w0 = gathered(1)
    u1 = w0_ref[...] * diag_ref[...] + expand(rows_w0)
    sum_over_lines(0)
    w1 = apply(1, u1)

    send_coefficients(2, coefficients(w1))
    rows_w1 = gathered(2)
    value = summed(0)
    g00 = value(1)
    alpha0 = value(0) / g00
    z1 = u0_ref[...] - alpha0 * u1
    s1 = w0_ref[...] - alpha0 * w1
    z1_ref[...] = z1
    s1_ref[...] = s1
    q = alpha0 * s1 * diag_ref[...] + expand([alpha0 * (a - alpha0 * b) for a, b in zip(rows_w0, rows_w1)])
    v = apply(2, q)

    r1 = rhs_ref[...] - alpha0 * w0_ref[...]
    u0, z1, s1 = u0_ref[...], z1_ref[...], s1_ref[...]
    sum_over_group(1, [total(u0 * s1), total(u0 * v), total(z1 * s1), total(z1 * v), total(q * v), total(z1 * r1), total(q * r1)])
    sum_over_lines(1)
    value = summed(1)
    g01, g02, g11, g12, g22, b1, b2 = [value(j) for j in range(7)]
    l10 = g01 / g00
    l20 = g02 / g00
    d1 = g11 - l10 * g01
    e12 = g12 - l20 * g01
    l21 = e12 / d1
    d2 = g22 - l20 * g02 - l21 * e12
    c2 = (b2 - l21 * b1) / d2
    c1 = b1 / d1 - l21 * c2
    c0 = -(l10 * c1 + l20 * c2)
    x_ref[...] = (alpha0 + c0) * u0 + c1 * z1 + c2 * q
    res_ref[...] = r1 - c0 * w0_ref[...] - c1 * s1 - c2 * v


def conjugate_gradients(n_gx, n_gy, *args):
    tile = args[0].shape
    vectors, _, lanes = args[5].shape
    field = VMEM(tile, jnp.float32)
    dma = pltpu.SemaphoreType.DMA
    f32 = jnp.float32
    return pl.pallas_call(
        functools.partial(cg_kernel, n_gx, n_gy),
        out_shape=(jax.ShapeDtypeStruct(tile, f32),) * 2,
        in_specs=[pl.BlockSpec(memory_space=VMEM)] * 7,
        out_specs=(pl.BlockSpec(memory_space=VMEM),) * 2,
        scratch_shapes=[field] * 7
        + [
            VMEM((vectors, lanes), f32),
            VMEM((3, 1, lanes), f32),
            VMEM((3, n_gx, 1, lanes), f32),
            VMEM((2, 2, 1, lanes), f32),
            VMEM((2, n_gx, 1, lanes), f32),
            VMEM((2, n_gy, 1, lanes), f32),
            VMEM((3, 4, 1, lanes), f32),
            VMEM((3, 4, 1, lanes), f32),
            VMEM((2, 1, lanes), f32),
            VMEM((2, 1, lanes), f32),
            dma((3,)), dma((3,)), dma((2,)), dma((2,)), dma((2,)), dma((2,)),
            dma((3, 4)), dma((3, 4)), dma((2,)), dma((2,)),
        ],
        compiler_params=pltpu.CompilerParams(collective_id=1, has_side_effects=True, vmem_limit_bytes=32 * 2**20),
        name="conjugate_gradients",
    )(*args)


def body(n_gx, n_gy, right_side, shift, face_x, face_y, ice_mask, deflation, coarse_matrix):
    whole = gather(coarse_matrix[0])
    rows = inverse_rows(whole, coarse_matrix.shape[1])
    return conjugate_gradients(n_gx, n_gy, right_side, shift, face_x, face_y, ice_mask, deflation, rows)


def solution(mesh):
    in_specs = (
        P("gx", "gy"),
        P("gx", "gy"),
        P("gx", "gy"),
        P("gx", "gy"),
        P("gx", "gy"),
        P(None, "gx", "gy"),
        P("gy", "gx", None),
    )
    out_specs = (P("gx", "gy"), P("gx", "gy"))
    run = functools.partial(body, mesh.shape["gx"], mesh.shape["gy"])
    return jax.shard_map(run, mesh=mesh, in_specs=in_specs, out_specs=out_specs, check_vma=False)
```

```python
import functools

import jax
import jax.numpy as jnp
from jax import lax
from jax.experimental import pallas as pl
from jax.experimental.pallas import tpu as pltpu
from jax.sharding import PartitionSpec as P

HIGH = lax.Precision.HIGHEST
MESH = pl.DeviceIdType.MESH
VMEM = pltpu.VMEM
SIDE = 4
B = 128
W = 8
TILES = B // W
GROUP = 4


def along_gx(index):
    return {"gx": index}


def gather_kernel(own_ref, whole, local_sem, send_sem, near_sem, far_sem, core_sem, core_send):
    rows = own_ref.shape[0]
    half = rows // 2
    me = lax.axis_index("gx")
    core = lax.rem(me, 2)
    y = lax.rem(me // 2, SIDE)
    x = me // (2 * SIDE)

    def at(a, b):
        xx = lax.rem(x + core * a + (1 - core) * b + 2 * SIDE, SIDE)
        yy = lax.rem(y + (1 - core) * a + core * b + 2 * SIDE, SIDE)
        return (xx * SIDE + yy) * 2 + core

    other = me + 1 - 2 * core
    peers = [at(1, 0), at(-1, 0), at(0, 1), at(0, -1), other]
    barrier = pltpu.get_barrier_semaphore()
    for peer in peers:
        pl.semaphore_signal(barrier, inc=1, device_id=along_gx(peer), device_id_type=MESH)
    pl.semaphore_wait(barrier, len(peers))

    def block(a, b, part=None):
        start = at(a, b) * rows
        if part is None:
            return whole.at[pl.ds(pl.multiple_of(start, rows), rows), :]
        return whole.at[pl.ds(pl.multiple_of(start + part * half, half), half), :]

    sent = []

    def send(a, b, part, peer, sem):
        source = own_ref if (a, b) == (0, 0) else block(a, b, part)
        copy = pltpu.make_async_remote_copy(
            src_ref=source,
            dst_ref=block(a, b, part),
            send_sem=send_sem.at[len(sent)],
            recv_sem=sem,
            device_id=along_gx(peer),
            device_id_type=MESH,
        )
        copy.start()
        sent.append(copy)

    crossed = []

    def cross(a, b):
        source = own_ref if (a, b) == (0, 0) else block(a, b)
        i = len(crossed)
        copy = pltpu.make_async_remote_copy(
            src_ref=source,
            dst_ref=block(a, b),
            send_sem=core_send.at[i],
            recv_sem=core_sem.at[i],
            device_id=along_gx(other),
            device_id_type=MESH,
        )
        copy.start()
        crossed.append(copy)

    def arrived(a, b, part, sem):
        ref = block(a, b, part)
        pltpu.make_async_copy(ref, ref, sem).wait()

    def spread(a):
        send(a, 0, None, peers[2], far_sem.at[a % SIDE, 0])
        send(a, 0, None, peers[3], far_sem.at[a % SIDE, 1])

    def spread_on(a):
        arrived(a, -1, None, far_sem.at[a % SIDE, 0])
        send(a, -1, 0, peers[2], far_sem.at[a % SIDE, 2])
        arrived(a, 1, None, far_sem.at[a % SIDE, 1])
        send(a, 1, 1, peers[3], far_sem.at[a % SIDE, 3])
        cross(a, -1)
        cross(a, 1)

    def spread_end(a):
        arrived(a, 2, 0, far_sem.at[a % SIDE, 2])
        arrived(a, 2, 1, far_sem.at[a % SIDE, 3])
        cross(a, 2)

    send(0, 0, None, peers[0], near_sem.at[0])
    send(0, 0, None, peers[1], near_sem.at[1])
    spread(0)
    cross(0, 0)
    mine = pltpu.make_async_copy(own_ref, block(0, 0), local_sem)
    mine.start()
    arrived(-1, 0, None, near_sem.at[0])
    send(-1, 0, 0, peers[0], near_sem.at[2])
    spread(-1)
    arrived(1, 0, None, near_sem.at[1])
    send(1, 0, 1, peers[1], near_sem.at[3])
    spread(1)
    cross(-1, 0)
    cross(1, 0)
    spread_on(0)
    arrived(2, 0, 0, near_sem.at[2])
    arrived(2, 0, 1, near_sem.at[3])
    spread(2)
    cross(2, 0)
    spread_on(-1)
    spread_end(0)
    spread_on(1)
    spread_end(-1)
    spread_on(2)
    spread_end(1)
    spread_end(2)
    mine.wait()
    for copy in sent:
        copy.wait_send()
    for copy in crossed:
        copy.wait()


def gather(own):
    rows, columns = own.shape
    return pl.pallas_call(
        gather_kernel,
        out_shape=jax.ShapeDtypeStruct((32 * rows, columns), own.dtype),
        in_specs=[pl.BlockSpec(memory_space=VMEM)],
        out_specs=pl.BlockSpec(memory_space=pl.ANY),
        scratch_shapes=[
            pltpu.SemaphoreType.DMA,
            pltpu.SemaphoreType.DMA((20,)),
            pltpu.SemaphoreType.DMA((4,)),
            pltpu.SemaphoreType.DMA((4, 4)),
            pltpu.SemaphoreType.DMA((16,)),
            pltpu.SemaphoreType.DMA((16,)),
        ],
        compiler_params=pltpu.CompilerParams(collective_id=0, has_side_effects=True),
        name="gather",
    )(own)


def dot(a, b, contract=(1, 0)):
    dims = (((contract[0],), (contract[1],)), ((), ()))
    return lax.dot_general(a, b, dims, precision=HIGH, preferred_element_type=jnp.float32)


def invert_block(load, ones, between):
    sub = lax.broadcasted_iota(jnp.int32, (W, B), 0)
    lane = lax.broadcasted_iota(jnp.int32, (W, B), 1)
    zero = jnp.zeros((W, B), jnp.float32)
    a = [load(i) for i in range(TILES)]
    low, scaled = [], []

    def row(t, j):
        return jnp.broadcast_to(t[j : j + 1, :], (W, B))

    def column(t, j):
        return jnp.broadcast_to(t[:, j : j + 1], (W, B))

    for g in range(0, TILES, GROUP):
        pair = range(g, g + GROUP)
        for i in pair:
            low.append(jnp.where(lane < g * W, a[i], jnp.where(lane == i * W + sub, 1.0, 0.0)))
        for p in pair:
            t = a[p]
            own = (lane >= p * W) & (lane < (p + 1) * W)
            others = [i for i in pair if i != p]
            b = [column(t, p * W + j) * ones for j in range(W)]
            c = {(i, j): column(a[i], p * W + j) for i in others for j in range(W)}
            t = jnp.where(own, jnp.where(lane == p * W + sub, 1.0, 0.0), t)
            for j in range(0, W, 2):
                k = j + 1
                first, both, second = row(b[j], j), row(b[k], j), row(b[k], k)
                f = 1.0 / (first * second - both * both)
                two = (sub == j) | (sub == k)
                m, n = jnp.where(two, 0.0, b[j]), jnp.where(two, 0.0, b[k])

                def eliminate(v):
                    vj, vk = row(v, j), row(v, k)
                    nj = (second * vj - both * vk) * f
                    nk = (first * vk - both * vj) * f
                    return jnp.where(sub == j, nj, jnp.where(sub == k, nk, v - (m * nj + n * nk)))

                b = [eliminate(b[q]) if q > k else None for q in range(W)]
                t = eliminate(t)
            rows = [row(t, j) for j in range(W)]
            for i in others:
                s = [c[i, 2 * h] * rows[2 * h] + c[i, 2 * h + 1] * rows[2 * h + 1] for h in range(W // 2)]
                a[i] = jnp.where(own, 0.0, a[i]) - ((s[0] + s[1]) + (s[2] + s[3]))
            a[p] = t
        end = (g + GROUP) * W
        scaled += [jnp.where(lane < end, a[i], 0.0) for i in pair]
        if g + GROUP < TILES:
            inside = (lane >= g * W) & (lane < end)
            weights = [zero] * g + [a[i] for i in pair] + [zero] * (TILES - g - GROUP)
            change = dot(jnp.concatenate(a[g + GROUP :], 0), jnp.concatenate(weights, 0))
            for n, i in enumerate(range(g + GROUP, TILES)):
                a[i] = jnp.where(inside, 0.0, a[i]) - change[n * W : (n + 1) * W]
        between(g // GROUP)
    return dot(jnp.concatenate(low, 0), jnp.concatenate(scaled, 0), (0, 0))


def inverse_kernel(e_ref, t_ref, e, panels, unit, scale):
    own, size = t_ref.shape
    blocks = size // B
    first = lax.axis_index("gx") * own
    at = lax.broadcasted_iota(jnp.int32, (own, size), 1) - lax.broadcasted_iota(jnp.int32, (own, size), 0)
    eye = lax.broadcasted_iota(jnp.int32, (B, B), 0) == lax.broadcasted_iota(jnp.int32, (B, B), 1)
    waiting = []

    def between(i):
        left = TILES // GROUP - 1 - i
        count = len(waiting) if left == 0 else -(-len(waiting) // (left + 1))
        for _ in range(count):
            waiting.pop(0)()

    def span(k):
        return slice(k * B, (k + 1) * B)

    by_row = []
    for k in range(blocks):
        diagonal = jnp.where(eye, e_ref[span(k), span(k)], 0.0)
        scale[:, span(k)] = lax.rsqrt(jnp.sum(diagonal, axis=0, keepdims=True))
        by_row.append(lax.rsqrt(jnp.sum(diagonal, axis=1, keepdims=True)))
    for k in range(blocks):
        upper = slice(k * B, size)
        e[span(k), upper] = e_ref[span(k), upper] * by_row[k] * scale[:, upper]
    unit[...] = jnp.where(at == first, scale[...], 0.0)
    ones = jnp.broadcast_to(jnp.minimum(scale[:, :B] + 1.0, 1.0), (W, B))

    def trail(k, i, columns):
        e[span(i), columns] -= dot(e[span(k), span(i)], panels[span(k), columns], (0, 0))

    for k in range(blocks):
        d = invert_block(lambda i: e[k * B + i * W : k * B + (i + 1) * W, span(k)], ones, between)
        if k + 1 < blocks:
            after = slice((k + 1) * B, size)
            panels[span(k), span(k + 1)] = dot(d, e[span(k), span(k + 1)])
            trail(k, k + 1, span(k + 1))

            def rest(k=k, d=d):
                far = slice((k + 2) * B, size)
                panels[span(k), far] = dot(d, e[span(k), far])

            def across(k=k, after=after):
                unit[:, after] -= dot(unit[:, span(k)], panels[span(k), after])

            if k + 2 < blocks:
                waiting.append(rest)
                for i in range(k + 1, blocks):
                    for j in range(max(i, k + 2), blocks, 2):
                        columns = slice(j * B, min(j + 2, blocks) * B)
                        waiting.append(lambda k=k, i=i, columns=columns: trail(k, i, columns))
            waiting.append(across)
        waiting.append(lambda k=k, d=d: t_ref.__setitem__((slice(None), span(k)), dot(unit[:, span(k)], d)))
    for work in waiting:
        work()
    for k in reversed(range(blocks - 1)):
        after = slice((k + 1) * B, size)
        t_ref[:, span(k)] -= dot(t_ref[:, after], panels[span(k), after], (1, 1))
    t_ref[...] *= scale[...]


def inverse_rows(whole, own):
    size = whole.shape[0]
    return pl.pallas_call(
        inverse_kernel,
        out_shape=jax.ShapeDtypeStruct((own, size), jnp.float32),
        in_specs=[pl.BlockSpec(memory_space=VMEM)],
        out_specs=pl.BlockSpec(memory_space=VMEM),
        scratch_shapes=[
            VMEM((size, size), jnp.float32),
            VMEM((size, size), jnp.float32),
            VMEM((own, size), jnp.float32),
            VMEM((1, size), jnp.float32),
        ],
        compiler_params=pltpu.CompilerParams(vmem_limit_bytes=48 * 2**20),
        name="inverse_rows",
    )(whole)


def total(a):
    return jnp.sum(jnp.sum(a, axis=0, keepdims=True), axis=1, keepdims=True)


def cg_kernel(
    n_gx, n_gy, rhs_ref, shift_ref, fx_ref, fy_ref, mask_ref, v_ref, t_ref, x_ref, res_ref,
    u0_ref, w0_ref, z1_ref, s1_ref, cu_ref, cl_ref, diag_ref, y_ref,
    msg, coef, sums, group, line, edge_out, edge_in, face_out, face_in,
    coef_send, coef_recv, group_send, group_recv, line_send, line_recv, edge_send, edge_recv, face_send, face_recv,
):
    vectors, cx_n, cy_n = v_ref.shape
    gx, gy = lax.axis_index("gx"), lax.axis_index("gy")
    lane1 = lax.broadcasted_iota(jnp.int32, (1, cy_n), 1)
    row2 = lax.broadcasted_iota(jnp.int32, (cx_n, cy_n), 0)
    lane2 = lax.broadcasted_iota(jnp.int32, (cx_n, cy_n), 1)
    eye = row2 == lane2

    def along(axis, count, step):
        return {axis: lax.rem(lax.axis_index(axis) + step, count)}

    below, above = along("gx", n_gx, 1), along("gx", n_gx, n_gx - 1)
    right, left = along("gy", n_gy, 1), along("gy", n_gy, n_gy - 1)

    barrier = pltpu.get_barrier_semaphore()
    for axis, count in (("gx", n_gx), ("gy", n_gy)):

        def greet(step, carry, axis=axis, count=count):
            pl.semaphore_signal(barrier, inc=1, device_id=along(axis, count, step), device_id_type=MESH)
            return carry

        lax.fori_loop(1, count, greet, 0)

    mask = mask_ref[...].astype(jnp.float32)
    cx = fx_ref[...] * mask
    cy = fy_ref[...] * mask
    self_term = shift_ref[...] * mask + (1.0 - mask)

    def as_row(column):
        return jnp.sum(jnp.where(eye, column, 0.0), axis=0, keepdims=True)

    def as_column(row):
        return jnp.sum(jnp.where(eye, row, 0.0), axis=1, keepdims=True)

    face_out[0] = cx[cx_n - 1 :, :]
    face_out[1] = as_row(cy[:, cy_n - 1 :])

    def coefficients(field):
        parts = jnp.sum(v_ref[...] * field[None], axis=1)
        column = jnp.sum(parts, axis=1, keepdims=True)
        place = lax.rem(gx, cy_n // vectors) * vectors + lax.broadcasted_iota(jnp.int32, (vectors, cy_n), 0)
        here = lax.broadcasted_iota(jnp.int32, (vectors, cy_n), 1) == place
        return jnp.sum(jnp.where(here, column, 0.0), axis=0, keepdims=True)

    first = coefficients(rhs_ref[...])

    pl.semaphore_wait(barrier, n_gx + n_gy - 2)

    faces = []
    for i, (peer, name) in enumerate(((below, "x"), (right, "y"))):
        copy = pltpu.make_async_remote_copy(
            src_ref=face_out.at[i], dst_ref=face_in.at[i], send_sem=face_send.at[i], recv_sem=face_recv.at[i],
            device_id=peer, device_id_type=MESH,
        )
        copy.start()
        faces.append(copy)

    def share(source, slots, axis, count, send, recv):
        me = lax.axis_index(axis)
        slots[me] = source[...]

        for step in sorted(range(1, count), key=lambda s: abs(s - count // 2)):
            pltpu.make_async_remote_copy(
                src_ref=source, dst_ref=slots.at[me], send_sem=send, recv_sem=recv,
                device_id=along(axis, count, step), device_id_type=MESH,
            ).start()

    def shared(slots, count, send, recv):
        others = slots.at[pl.ds(0, count - 1)]
        pltpu.make_async_copy(others, others, recv).wait()
        pltpu.make_async_copy(others, others, send).wait()

    def send_coefficients(i, row):
        msg[i] = row
        share(msg.at[i], coef.at[i], "gx", n_gx, coef_send.at[i], coef_recv.at[i])

    def gathered(i):
        shared(coef.at[i], n_gx, coef_send.at[i], coef_recv.at[i])
        each = cy_n // vectors
        return [sum(coef[i, p * each + j] for j in range(1, each)) + coef[i, p * each] for p in range(n_gx // each)]

    def expand(rows):
        acc = sum(t_ref[:, p * cy_n : (p + 1) * cy_n] * row for p, row in enumerate(rows))
        y_ref[...] = jnp.broadcast_to(jnp.sum(acc, axis=1, keepdims=True), (vectors, cy_n))
        out = v_ref[0] * y_ref[0:1, :]
        for k in range(1, vectors):
            out = out + v_ref[k] * y_ref[k : k + 1, :]
        return out

    def apply(i, field):
        edge_out[i, 0] = field[cx_n - 1 :, :]
        edge_out[i, 1] = field[0:1, :]
        edge_out[i, 2] = as_row(field[:, cy_n - 1 :])
        edge_out[i, 3] = as_row(field[:, 0:1])
        copies = []
        for j, peer in enumerate((below, above, right, left)):
            copy = pltpu.make_async_remote_copy(
                src_ref=edge_out.at[i, j], dst_ref=edge_in.at[i, j],
                send_sem=edge_send.at[i, j], recv_sem=edge_recv.at[i, j],
                device_id=peer, device_id_type=MESH,
            )
            copy.start()
            copies.append(copy)
        down = pltpu.roll(field, cx_n - 1, 0)
        up = pltpu.roll(field, 1, 0)
        to_right = pltpu.roll(field, cy_n - 1, 1)
        to_left = pltpu.roll(field, 1, 1)
        for copy in copies:
            copy.wait()
        zero = jnp.zeros((1, cy_n), jnp.float32)
        from_above = jnp.where(gx > 0, edge_in[i, 0], zero)
        from_below = jnp.where(gx < n_gx - 1, edge_in[i, 1], zero)
        from_left = jnp.where(gy > 0, edge_in[i, 2], zero)
        from_right = jnp.where(gy < n_gy - 1, edge_in[i, 3], zero)
        down = jnp.where(row2 == cx_n - 1, from_below, down)
        up = jnp.where(row2 == 0, from_above, up)
        to_right = jnp.where(lane2 == cy_n - 1, as_column(from_right), to_right)
        to_left = jnp.where(lane2 == 0, as_column(from_left), to_left)
        mask = mask_ref[...].astype(jnp.float32)
        self_term = shift_ref[...] * mask + (1.0 - mask)
        return (
            self_term * field
            + fx_ref[...] * mask * (field - down)
            + cu_ref[...] * (field - up)
            + fy_ref[...] * mask * (field - to_right)
            + cl_ref[...] * (field - to_left)
        )

    def packed(values):
        row = jnp.zeros((1, cy_n), jnp.float32)
        for i, value in enumerate(values):
            row = jnp.where(lane1 == i, value, row)
        return row

    def sum_over_group(i, values):
        sums[i, 0] = packed(values)
        share(sums.at[i, 0], group.at[i], "gx", n_gx, group_send.at[i], group_recv.at[i])

    def sum_over_lines(i):
        shared(group.at[i], n_gx, group_send.at[i], group_recv.at[i])
        sums[i, 1] = sum(group[i, d] for d in range(1, n_gx)) + group[i, 0]
        share(sums.at[i, 1], line.at[i], "gy", n_gy, line_send.at[i], line_recv.at[i])

    def summed(i):
        shared(line.at[i], n_gy, line_send.at[i], line_recv.at[i])
        row = sum(line[i, d] for d in range(1, n_gy)) + line[i, 0]

        def value(j):
            return jnp.sum(jnp.where(lane1 == j, row, 0.0), axis=1, keepdims=True)

        return value

    send_coefficients(0, first)
    for copy in faces:
        copy.wait()
    upper = jnp.where(gx > 0, face_in[0], jnp.zeros((1, cy_n), jnp.float32))
    beside = jnp.where(gy > 0, face_in[1], jnp.zeros((1, cy_n), jnp.float32))
    cu = jnp.where(row2 == 0, upper, pltpu.roll(cx, 1, 0))
    cl = jnp.where(lane2 == 0, as_column(beside), pltpu.roll(cy, 1, 1))
    cu_ref[...] = cu
    cl_ref[...] = cl
    inverse_diag = 1.0 / (self_term + cx + cu + cy + cl)
    diag_ref[...] = inverse_diag
    u0 = rhs_ref[...] * inverse_diag + expand(gathered(0))
    u0_ref[...] = u0
    w0 = apply(0, u0)
    w0_ref[...] = w0

    send_coefficients(1, coefficients(w0))
    sum_over_group(0, [total(rhs_ref[...] * u0), total(u0 * w0)])
    rows_w0 = gathered(1)
    u1 = w0_ref[...] * diag_ref[...] + expand(rows_w0)
    sum_over_lines(0)
    w1 = apply(1, u1)

    send_coefficients(2, coefficients(w1))
    rows_w1 = gathered(2)
    value = summed(0)
    g00 = value(1)
    alpha0 = value(0) / g00
    z1 = u0_ref[...] - alpha0 * u1
    s1 = w0_ref[...] - alpha0 * w1
    z1_ref[...] = z1
    s1_ref[...] = s1
    q = alpha0 * s1 * diag_ref[...] + expand([alpha0 * (a - alpha0 * b) for a, b in zip(rows_w0, rows_w1)])
    v = apply(2, q)

    r1 = rhs_ref[...] - alpha0 * w0_ref[...]
    u0, z1, s1 = u0_ref[...], z1_ref[...], s1_ref[...]
    sum_over_group(1, [total(u0 * s1), total(u0 * v), total(z1 * s1), total(z1 * v), total(q * v), total(z1 * r1), total(q * r1)])
    sum_over_lines(1)
    value = summed(1)
    g01, g02, g11, g12, g22, b1, b2 = [value(j) for j in range(7)]
    l10 = g01 / g00
    l20 = g02 / g00
    d1 = g11 - l10 * g01
    e12 = g12 - l20 * g01
    l21 = e12 / d1
    d2 = g22 - l20 * g02 - l21 * e12
    c2 = (b2 - l21 * b1) / d2
    c1 = b1 / d1 - l21 * c2
    c0 = -(l10 * c1 + l20 * c2)
    x_ref[...] = (alpha0 + c0) * u0 + c1 * z1 + c2 * q
    res_ref[...] = r1 - c0 * w0_ref[...] - c1 * s1 - c2 * v


def conjugate_gradients(n_gx, n_gy, *args):
    tile = args[0].shape
    vectors, _, lanes = args[5].shape
    field = VMEM(tile, jnp.float32)
    dma = pltpu.SemaphoreType.DMA
    f32 = jnp.float32
    return pl.pallas_call(
        functools.partial(cg_kernel, n_gx, n_gy),
        out_shape=(jax.ShapeDtypeStruct(tile, f32),) * 2,
        in_specs=[pl.BlockSpec(memory_space=VMEM)] * 7,
        out_specs=(pl.BlockSpec(memory_space=VMEM),) * 2,
        scratch_shapes=[field] * 7
        + [
            VMEM((vectors, lanes), f32),
            VMEM((3, 1, lanes), f32),
            VMEM((3, n_gx, 1, lanes), f32),
            VMEM((2, 2, 1, lanes), f32),
            VMEM((2, n_gx, 1, lanes), f32),
            VMEM((2, n_gy, 1, lanes), f32),
            VMEM((3, 4, 1, lanes), f32),
            VMEM((3, 4, 1, lanes), f32),
            VMEM((2, 1, lanes), f32),
            VMEM((2, 1, lanes), f32),
            dma((3,)), dma((3,)), dma((2,)), dma((2,)), dma((2,)), dma((2,)),
            dma((3, 4)), dma((3, 4)), dma((2,)), dma((2,)),
        ],
        compiler_params=pltpu.CompilerParams(collective_id=1, has_side_effects=True, vmem_limit_bytes=32 * 2**20),
        name="conjugate_gradients",
    )(*args)


def body(n_gx, n_gy, right_side, shift, face_x, face_y, ice_mask, deflation, coarse_matrix):
    whole = gather(coarse_matrix[0])
    rows = inverse_rows(whole, coarse_matrix.shape[1])
    return conjugate_gradients(n_gx, n_gy, right_side, shift, face_x, face_y, ice_mask, deflation, rows)


def solution(mesh):
    in_specs = (
        P("gx", "gy"),
        P("gx", "gy"),
        P("gx", "gy"),
        P("gx", "gy"),
        P("gx", "gy"),
        P(None, "gx", "gy"),
        P("gy", "gx", None),
    )
    out_specs = (P("gx", "gy"), P("gx", "gy"))
    run = functools.partial(body, mesh.shape["gx"], mesh.shape["gy"])
    return jax.shard_map(run, mesh=mesh, in_specs=in_specs, out_specs=out_specs, check_vma=False)
```

```python
import functools

import jax
import jax.numpy as jnp
from jax import lax
from jax.experimental import pallas as pl
from jax.experimental.pallas import tpu as pltpu
from jax.sharding import PartitionSpec as P

HIGH = lax.Precision.HIGHEST
MESH = pl.DeviceIdType.MESH
VMEM = pltpu.VMEM
SIDE = 4
B = 128
W = 8
TILES = B // W
GROUP = 2


def along_gx(index):
    return {"gx": index}


def gather_kernel(own_ref, whole, local_sem, send_sem, near_sem, far_sem, core_sem, core_send):
    rows = own_ref.shape[0]
    half = rows // 2
    me = lax.axis_index("gx")
    core = lax.rem(me, 2)
    y = lax.rem(me // 2, SIDE)
    x = me // (2 * SIDE)

    def at(a, b):
        xx = lax.rem(x + core * a + (1 - core) * b + 2 * SIDE, SIDE)
        yy = lax.rem(y + (1 - core) * a + core * b + 2 * SIDE, SIDE)
        return (xx * SIDE + yy) * 2 + core

    other = me + 1 - 2 * core
    peers = [at(1, 0), at(-1, 0), at(0, 1), at(0, -1), other]
    barrier = pltpu.get_barrier_semaphore()
    for peer in peers:
        pl.semaphore_signal(barrier, inc=1, device_id=along_gx(peer), device_id_type=MESH)
    pl.semaphore_wait(barrier, len(peers))

    def block(a, b, part=None):
        start = at(a, b) * rows
        if part is None:
            return whole.at[pl.ds(pl.multiple_of(start, rows), rows), :]
        return whole.at[pl.ds(pl.multiple_of(start + part * half, half), half), :]

    sent = []

    def send(a, b, part, peer, sem):
        source = own_ref if (a, b) == (0, 0) else block(a, b, part)
        copy = pltpu.make_async_remote_copy(
            src_ref=source,
            dst_ref=block(a, b, part),
            send_sem=send_sem.at[len(sent)],
            recv_sem=sem,
            device_id=along_gx(peer),
            device_id_type=MESH,
        )
        copy.start()
        sent.append(copy)

    crossed = []

    def cross(a, b):
        source = own_ref if (a, b) == (0, 0) else block(a, b)
        i = len(crossed)
        copy = pltpu.make_async_remote_copy(
            src_ref=source,
            dst_ref=block(a, b),
            send_sem=core_send.at[i],
            recv_sem=core_sem.at[i],
            device_id=along_gx(other),
            device_id_type=MESH,
        )
        copy.start()
        crossed.append(copy)

    def arrived(a, b, part, sem):
        ref = block(a, b, part)
        pltpu.make_async_copy(ref, ref, sem).wait()

    def spread(a):
        send(a, 0, None, peers[2], far_sem.at[a % SIDE, 0])
        send(a, 0, None, peers[3], far_sem.at[a % SIDE, 1])

    def spread_on(a):
        arrived(a, -1, None, far_sem.at[a % SIDE, 0])
        send(a, -1, 0, peers[2], far_sem.at[a % SIDE, 2])
        arrived(a, 1, None, far_sem.at[a % SIDE, 1])
        send(a, 1, 1, peers[3], far_sem.at[a % SIDE, 3])
        cross(a, -1)
        cross(a, 1)

    def spread_end(a):
        arrived(a, 2, 0, far_sem.at[a % SIDE, 2])
        arrived(a, 2, 1, far_sem.at[a % SIDE, 3])
        cross(a, 2)

    send(0, 0, None, peers[0], near_sem.at[0])
    send(0, 0, None, peers[1], near_sem.at[1])
    spread(0)
    cross(0, 0)
    mine = pltpu.make_async_copy(own_ref, block(0, 0), local_sem)
    mine.start()
    arrived(-1, 0, None, near_sem.at[0])
    send(-1, 0, 0, peers[0], near_sem.at[2])
    spread(-1)
    arrived(1, 0, None, near_sem.at[1])
    send(1, 0, 1, peers[1], near_sem.at[3])
    spread(1)
    cross(-1, 0)
    cross(1, 0)
    spread_on(0)
    arrived(2, 0, 0, near_sem.at[2])
    arrived(2, 0, 1, near_sem.at[3])
    spread(2)
    cross(2, 0)
    spread_on(-1)
    spread_end(0)
    spread_on(1)
    spread_end(-1)
    spread_on(2)
    spread_end(1)
    spread_end(2)
    mine.wait()
    for copy in sent:
        copy.wait_send()
    for copy in crossed:
        copy.wait()


def gather(own):
    rows, columns = own.shape
    return pl.pallas_call(
        gather_kernel,
        out_shape=jax.ShapeDtypeStruct((32 * rows, columns), own.dtype),
        in_specs=[pl.BlockSpec(memory_space=VMEM)],
        out_specs=pl.BlockSpec(memory_space=pl.ANY),
        scratch_shapes=[
            pltpu.SemaphoreType.DMA,
            pltpu.SemaphoreType.DMA((20,)),
            pltpu.SemaphoreType.DMA((4,)),
            pltpu.SemaphoreType.DMA((4, 4)),
            pltpu.SemaphoreType.DMA((16,)),
            pltpu.SemaphoreType.DMA((16,)),
        ],
        compiler_params=pltpu.CompilerParams(collective_id=0, has_side_effects=True),
        name="gather",
    )(own)


def dot(a, b, contract=(1, 0)):
    dims = (((contract[0],), (contract[1],)), ((), ()))
    return lax.dot_general(a, b, dims, precision=HIGH, preferred_element_type=jnp.float32)


def invert_block(load, ones, between):
    sub = lax.broadcasted_iota(jnp.int32, (W, B), 0)
    lane = lax.broadcasted_iota(jnp.int32, (W, B), 1)
    zero = jnp.zeros((W, B), jnp.float32)
    a = [load(i) for i in range(TILES)]
    low, scaled = [], []

    def row(t, j):
        return jnp.broadcast_to(t[j : j + 1, :], (W, B))

    def column(t, j):
        return jnp.broadcast_to(t[:, j : j + 1], (W, B))

    for g in range(0, TILES, GROUP):
        pair = range(g, g + GROUP)
        for i in pair:
            low.append(jnp.where(lane < g * W, a[i], jnp.where(lane == i * W + sub, 1.0, 0.0)))
        for p in pair:
            t = a[p]
            own = (lane >= p * W) & (lane < (p + 1) * W)
            others = [i for i in pair if i != p]
            b = [column(t, p * W + j) * ones for j in range(W)]
            c = {(i, j): column(a[i], p * W + j) for i in others for j in range(W)}
            t = jnp.where(own, jnp.where(lane == p * W + sub, 1.0, 0.0), t)
            for j in range(0, W, 2):
                k = j + 1
                first, both, second = row(b[j], j), row(b[k], j), row(b[k], k)
                f = 1.0 / (first * second - both * both)
                two = (sub == j) | (sub == k)
                m, n = jnp.where(two, 0.0, b[j]), jnp.where(two, 0.0, b[k])

                def eliminate(v):
                    vj, vk = row(v, j), row(v, k)
                    nj = (second * vj - both * vk) * f
                    nk = (first * vk - both * vj) * f
                    return jnp.where(sub == j, nj, jnp.where(sub == k, nk, v - (m * nj + n * nk)))

                b = [eliminate(b[q]) if q > k else None for q in range(W)]
                t = eliminate(t)
            rows = [row(t, j) for j in range(W)]
            for i in others:
                s = [c[i, 2 * h] * rows[2 * h] + c[i, 2 * h + 1] * rows[2 * h + 1] for h in range(W // 2)]
                a[i] = jnp.where(own, 0.0, a[i]) - ((s[0] + s[1]) + (s[2] + s[3]))
            a[p] = t
        end = (g + GROUP) * W
        scaled += [jnp.where(lane < end, a[i], 0.0) for i in pair]
        if g + GROUP < TILES:
            inside = (lane >= g * W) & (lane < end)
            weights = [zero] * g + [a[i] for i in pair] + [zero] * (TILES - g - GROUP)
            change = dot(jnp.concatenate(a[g + GROUP :], 0), jnp.concatenate(weights, 0))
            for n, i in enumerate(range(g + GROUP, TILES)):
                a[i] = jnp.where(inside, 0.0, a[i]) - change[n * W : (n + 1) * W]
        between(g // GROUP)
    return dot(jnp.concatenate(low, 0), jnp.concatenate(scaled, 0), (0, 0))


def inverse_kernel(e_ref, t_ref, e, panels, unit, scale):
    own, size = t_ref.shape
    blocks = size // B
    first = lax.axis_index("gx") * own
    at = lax.broadcasted_iota(jnp.int32, (own, size), 1) - lax.broadcasted_iota(jnp.int32, (own, size), 0)
    eye = lax.broadcasted_iota(jnp.int32, (B, B), 0) == lax.broadcasted_iota(jnp.int32, (B, B), 1)
    waiting = []

    def between(i):
        left = TILES // GROUP - 1 - i
        count = len(waiting) if left == 0 else -(-len(waiting) // (left + 1))
        for _ in range(count):
            waiting.pop(0)()

    def span(k):
        return slice(k * B, (k + 1) * B)

    by_row = []
    for k in range(blocks):
        diagonal = jnp.where(eye, e_ref[span(k), span(k)], 0.0)
        scale[:, span(k)] = lax.rsqrt(jnp.sum(diagonal, axis=0, keepdims=True))
        by_row.append(lax.rsqrt(jnp.sum(diagonal, axis=1, keepdims=True)))
    for k in range(blocks):
        upper = slice(k * B, size)
        e[span(k), upper] = e_ref[span(k), upper] * by_row[k] * scale[:, upper]
    unit[...] = jnp.where(at == first, scale[...], 0.0)
    ones = jnp.broadcast_to(jnp.minimum(scale[:, :B] + 1.0, 1.0), (W, B))

    def trail(k, i, columns):
        e[span(i), columns] -= dot(e[span(k), span(i)], panels[span(k), columns], (0, 0))

    for k in range(blocks):
        d = invert_block(lambda i: e[k * B + i * W : k * B + (i + 1) * W, span(k)], ones, between)
        if k + 1 < blocks:
            after = slice((k + 1) * B, size)
            panels[span(k), span(k + 1)] = dot(d, e[span(k), span(k + 1)])
            trail(k, k + 1, span(k + 1))

            def rest(k=k, d=d):
                far = slice((k + 2) * B, size)
                panels[span(k), far] = dot(d, e[span(k), far])

            def across(k=k, after=after):
                unit[:, after] -= dot(unit[:, span(k)], panels[span(k), after])

            if k + 2 < blocks:
                waiting.append(rest)
                for i in range(k + 1, blocks):
                    for j in range(max(i, k + 2), blocks, 2):
                        columns = slice(j * B, min(j + 2, blocks) * B)
                        waiting.append(lambda k=k, i=i, columns=columns: trail(k, i, columns))
            waiting.append(across)
        waiting.append(lambda k=k, d=d: t_ref.__setitem__((slice(None), span(k)), dot(unit[:, span(k)], d)))
    for work in waiting:
        work()
    for k in reversed(range(blocks - 1)):
        after = slice((k + 1) * B, size)
        t_ref[:, span(k)] -= dot(t_ref[:, after], panels[span(k), after], (1, 1))
    t_ref[...] *= scale[...]


def inverse_rows(whole, own):
    size = whole.shape[0]
    return pl.pallas_call(
        inverse_kernel,
        out_shape=jax.ShapeDtypeStruct((own, size), jnp.float32),
        in_specs=[pl.BlockSpec(memory_space=VMEM)],
        out_specs=pl.BlockSpec(memory_space=VMEM),
        scratch_shapes=[
            VMEM((size, size), jnp.float32),
            VMEM((size, size), jnp.float32),
            VMEM((own, size), jnp.float32),
            VMEM((1, size), jnp.float32),
        ],
        compiler_params=pltpu.CompilerParams(vmem_limit_bytes=48 * 2**20),
        name="inverse_rows",
    )(whole)


def total(a):
    return jnp.sum(jnp.sum(a, axis=0, keepdims=True), axis=1, keepdims=True)


def cg_kernel(
    n_gx, n_gy, rhs_ref, shift_ref, fx_ref, fy_ref, mask_ref, v_ref, t_ref, x_ref, res_ref,
    u0_ref, w0_ref, z1_ref, s1_ref, cu_ref, cl_ref, diag_ref, y_ref,
    msg, coef, sums, group, line, edge_out, edge_in, face_out, face_in,
    coef_send, coef_recv, group_send, group_recv, line_send, line_recv, edge_send, edge_recv, face_send, face_recv,
):
    vectors, cx_n, cy_n = v_ref.shape
    gx, gy = lax.axis_index("gx"), lax.axis_index("gy")
    lane1 = lax.broadcasted_iota(jnp.int32, (1, cy_n), 1)
    row2 = lax.broadcasted_iota(jnp.int32, (cx_n, cy_n), 0)
    lane2 = lax.broadcasted_iota(jnp.int32, (cx_n, cy_n), 1)
    eye = row2 == lane2

    def along(axis, count, step):
        return {axis: lax.rem(lax.axis_index(axis) + step, count)}

    below, above = along("gx", n_gx, 1), along("gx", n_gx, n_gx - 1)
    right, left = along("gy", n_gy, 1), along("gy", n_gy, n_gy - 1)

    barrier = pltpu.get_barrier_semaphore()
    for axis, count in (("gx", n_gx), ("gy", n_gy)):

        def greet(step, carry, axis=axis, count=count):
            pl.semaphore_signal(barrier, inc=1, device_id=along(axis, count, step), device_id_type=MESH)
            return carry

        lax.fori_loop(1, count, greet, 0)

    mask = mask_ref[...].astype(jnp.float32)
    cx = fx_ref[...] * mask
    cy = fy_ref[...] * mask
    self_term = shift_ref[...] * mask + (1.0 - mask)

    def as_row(column):
        return jnp.sum(jnp.where(eye, column, 0.0), axis=0, keepdims=True)

    def as_column(row):
        return jnp.sum(jnp.where(eye, row, 0.0), axis=1, keepdims=True)

    face_out[0] = cx[cx_n - 1 :, :]
    face_out[1] = as_row(cy[:, cy_n - 1 :])

    def coefficients(field):
        parts = jnp.sum(v_ref[...] * field[None], axis=1)
        column = jnp.sum(parts, axis=1, keepdims=True)
        place = lax.rem(gx, cy_n // vectors) * vectors + lax.broadcasted_iota(jnp.int32, (vectors, cy_n), 0)
        here = lax.broadcasted_iota(jnp.int32, (vectors, cy_n), 1) == place
        return jnp.sum(jnp.where(here, column, 0.0), axis=0, keepdims=True)

    first = coefficients(rhs_ref[...])

    pl.semaphore_wait(barrier, n_gx + n_gy - 2)

    faces = []
    for i, (peer, name) in enumerate(((below, "x"), (right, "y"))):
        copy = pltpu.make_async_remote_copy(
            src_ref=face_out.at[i], dst_ref=face_in.at[i], send_sem=face_send.at[i], recv_sem=face_recv.at[i],
            device_id=peer, device_id_type=MESH,
        )
        copy.start()
        faces.append(copy)

    def share(source, slots, axis, count, send, recv):
        me = lax.axis_index(axis)
        slots[me] = source[...]

        for step in sorted(range(1, count), key=lambda s: abs(s - count // 2)):
            pltpu.make_async_remote_copy(
                src_ref=source, dst_ref=slots.at[me], send_sem=send, recv_sem=recv,
                device_id=along(axis, count, step), device_id_type=MESH,
            ).start()

    def shared(slots, count, send, recv):
        others = slots.at[pl.ds(0, count - 1)]
        pltpu.make_async_copy(others, others, recv).wait()
        pltpu.make_async_copy(others, others, send).wait()

    def send_coefficients(i, row):
        msg[i] = row
        share(msg.at[i], coef.at[i], "gx", n_gx, coef_send.at[i], coef_recv.at[i])

    def gathered(i):
        shared(coef.at[i], n_gx, coef_send.at[i], coef_recv.at[i])
        each = cy_n // vectors
        return [sum(coef[i, p * each + j] for j in range(1, each)) + coef[i, p * each] for p in range(n_gx // each)]

    def expand(rows):
        acc = sum(t_ref[:, p * cy_n : (p + 1) * cy_n] * row for p, row in enumerate(rows))
        y_ref[...] = jnp.broadcast_to(jnp.sum(acc, axis=1, keepdims=True), (vectors, cy_n))
        out = v_ref[0] * y_ref[0:1, :]
        for k in range(1, vectors):
            out = out + v_ref[k] * y_ref[k : k + 1, :]
        return out

    def apply(i, field):
        edge_out[i, 0] = field[cx_n - 1 :, :]
        edge_out[i, 1] = field[0:1, :]
        edge_out[i, 2] = as_row(field[:, cy_n - 1 :])
        edge_out[i, 3] = as_row(field[:, 0:1])
        copies = []
        for j, peer in enumerate((below, above, right, left)):
            copy = pltpu.make_async_remote_copy(
                src_ref=edge_out.at[i, j], dst_ref=edge_in.at[i, j],
                send_sem=edge_send.at[i, j], recv_sem=edge_recv.at[i, j],
                device_id=peer, device_id_type=MESH,
            )
            copy.start()
            copies.append(copy)
        down = pltpu.roll(field, cx_n - 1, 0)
        up = pltpu.roll(field, 1, 0)
        to_right = pltpu.roll(field, cy_n - 1, 1)
        to_left = pltpu.roll(field, 1, 1)
        for copy in copies:
            copy.wait()
        zero = jnp.zeros((1, cy_n), jnp.float32)
        from_above = jnp.where(gx > 0, edge_in[i, 0], zero)
        from_below = jnp.where(gx < n_gx - 1, edge_in[i, 1], zero)
        from_left = jnp.where(gy > 0, edge_in[i, 2], zero)
        from_right = jnp.where(gy < n_gy - 1, edge_in[i, 3], zero)
        down = jnp.where(row2 == cx_n - 1, from_below, down)
        up = jnp.where(row2 == 0, from_above, up)
        to_right = jnp.where(lane2 == cy_n - 1, as_column(from_right), to_right)
        to_left = jnp.where(lane2 == 0, as_column(from_left), to_left)
        mask = mask_ref[...].astype(jnp.float32)
        self_term = shift_ref[...] * mask + (1.0 - mask)
        return (
            self_term * field
            + fx_ref[...] * mask * (field - down)
            + cu_ref[...] * (field - up)
            + fy_ref[...] * mask * (field - to_right)
            + cl_ref[...] * (field - to_left)
        )

    def packed(values):
        row = jnp.zeros((1, cy_n), jnp.float32)
        for i, value in enumerate(values):
            row = jnp.where(lane1 == i, value, row)
        return row

    def sum_over_group(i, values):
        sums[i, 0] = packed(values)
        share(sums.at[i, 0], group.at[i], "gx", n_gx, group_send.at[i], group_recv.at[i])

    def sum_over_lines(i):
        shared(group.at[i], n_gx, group_send.at[i], group_recv.at[i])
        sums[i, 1] = sum(group[i, d] for d in range(1, n_gx)) + group[i, 0]
        share(sums.at[i, 1], line.at[i], "gy", n_gy, line_send.at[i], line_recv.at[i])

    def summed(i):
        shared(line.at[i], n_gy, line_send.at[i], line_recv.at[i])
        row = sum(line[i, d] for d in range(1, n_gy)) + line[i, 0]

        def value(j):
            return jnp.sum(jnp.where(lane1 == j, row, 0.0), axis=1, keepdims=True)

        return value

    send_coefficients(0, first)
    for copy in faces:
        copy.wait()
    upper = jnp.where(gx > 0, face_in[0], jnp.zeros((1, cy_n), jnp.float32))
    beside = jnp.where(gy > 0, face_in[1], jnp.zeros((1, cy_n), jnp.float32))
    cu = jnp.where(row2 == 0, upper, pltpu.roll(cx, 1, 0))
    cl = jnp.where(lane2 == 0, as_column(beside), pltpu.roll(cy, 1, 1))
    cu_ref[...] = cu
    cl_ref[...] = cl
    inverse_diag = 1.0 / (self_term + cx + cu + cy + cl)
    diag_ref[...] = inverse_diag
    u0 = rhs_ref[...] * inverse_diag + expand(gathered(0))
    u0_ref[...] = u0
    w0 = apply(0, u0)
    w0_ref[...] = w0

    send_coefficients(1, coefficients(w0))
    sum_over_group(0, [total(rhs_ref[...] * u0), total(u0 * w0)])
    rows_w0 = gathered(1)
    u1 = w0_ref[...] * diag_ref[...] + expand(rows_w0)
    sum_over_lines(0)
    w1 = apply(1, u1)

    send_coefficients(2, coefficients(w1))
    rows_w1 = gathered(2)
    value = summed(0)
    g00 = value(1)
    alpha0 = value(0) / g00
    z1 = u0_ref[...] - alpha0 * u1
    s1 = w0_ref[...] - alpha0 * w1
    z1_ref[...] = z1
    s1_ref[...] = s1
    q = alpha0 * s1 * diag_ref[...] + expand([alpha0 * (a - alpha0 * b) for a, b in zip(rows_w0, rows_w1)])
    v = apply(2, q)

    r1 = rhs_ref[...] - alpha0 * w0_ref[...]
    u0, z1, s1 = u0_ref[...], z1_ref[...], s1_ref[...]
    sum_over_group(1, [total(u0 * s1), total(u0 * v), total(z1 * s1), total(z1 * v), total(q * v), total(z1 * r1), total(q * r1)])
    sum_over_lines(1)
    value = summed(1)
    g01, g02, g11, g12, g22, b1, b2 = [value(j) for j in range(7)]
    l10 = g01 / g00
    l20 = g02 / g00
    d1 = g11 - l10 * g01
    e12 = g12 - l20 * g01
    l21 = e12 / d1
    d2 = g22 - l20 * g02 - l21 * e12
    c2 = (b2 - l21 * b1) / d2
    c1 = b1 / d1 - l21 * c2
    c0 = -(l10 * c1 + l20 * c2)
    x_ref[...] = (alpha0 + c0) * u0 + c1 * z1 + c2 * q
    res_ref[...] = r1 - c0 * w0_ref[...] - c1 * s1 - c2 * v


def conjugate_gradients(n_gx, n_gy, *args):
    tile = args[0].shape
    vectors, _, lanes = args[5].shape
    field = VMEM(tile, jnp.float32)
    dma = pltpu.SemaphoreType.DMA
    f32 = jnp.float32
    return pl.pallas_call(
        functools.partial(cg_kernel, n_gx, n_gy),
        out_shape=(jax.ShapeDtypeStruct(tile, f32),) * 2,
        in_specs=[pl.BlockSpec(memory_space=VMEM)] * 7,
        out_specs=(pl.BlockSpec(memory_space=VMEM),) * 2,
        scratch_shapes=[field] * 7
        + [
            VMEM((vectors, lanes), f32),
            VMEM((3, 1, lanes), f32),
            VMEM((3, n_gx, 1, lanes), f32),
            VMEM((2, 2, 1, lanes), f32),
            VMEM((2, n_gx, 1, lanes), f32),
            VMEM((2, n_gy, 1, lanes), f32),
            VMEM((3, 4, 1, lanes), f32),
            VMEM((3, 4, 1, lanes), f32),
            VMEM((2, 1, lanes), f32),
            VMEM((2, 1, lanes), f32),
            dma((3,)), dma((3,)), dma((2,)), dma((2,)), dma((2,)), dma((2,)),
            dma((3, 4)), dma((3, 4)), dma((2,)), dma((2,)),
        ],
        compiler_params=pltpu.CompilerParams(collective_id=1, has_side_effects=True, vmem_limit_bytes=32 * 2**20),
        name="conjugate_gradients",
    )(*args)


def body(n_gx, n_gy, right_side, shift, face_x, face_y, ice_mask, deflation, coarse_matrix):
    whole = gather(coarse_matrix[0])
    rows = inverse_rows(whole, coarse_matrix.shape[1])
    return conjugate_gradients(n_gx, n_gy, right_side, shift, face_x, face_y, ice_mask, deflation, rows)


def solution(mesh):
    in_specs = (
        P("gx", "gy"),
        P("gx", "gy"),
        P("gx", "gy"),
        P("gx", "gy"),
        P("gx", "gy"),
        P(None, "gx", "gy"),
        P("gy", "gx", None),
    )
    out_specs = (P("gx", "gy"), P("gx", "gy"))
    run = functools.partial(body, mesh.shape["gx"], mesh.shape["gy"])
    return jax.shard_map(run, mesh=mesh, in_specs=in_specs, out_specs=out_specs, check_vma=False)
```
